128 devices in a mesh: depth: 8 (over x, core), tile: 16 (over z, y).
Axes of the slice: x: 4, y: 4, z: 4, core: 2. Of those that a mesh axis runs over, the one named last changes fastest.
Arguments:
- velocity: float32 [3, 128, 512, 2048], P(None, 'depth', 'tile'), may hold values from -6 to 6
- view_sign: int32 [16], P('tile'), may hold values from 0 to 1, as said below
- brick_flags: int32 [16, 128, 16], P('depth', 'tile'), may hold values from 0 to 1, as said below
Outputs:
- image_color: float32 [3, 512, 2048], P(None, 'tile', 'depth')
- image_alpha: float32 [512, 2048], P('tile', 'depth')
The draws below stay inside these ranges and needn't reach their ends.
Inputs may be any that keep to these rules, and one draw needn't show every extreme that they name: `view_sign`: 0 views a band of 32 image rows from the first index along the first dimension, 1 from its last; exactly half of the bands hold 1. `brick_flags`: 1 marks a brick that is rendered, 0 a brick that is treated as empty.
All inputs are finite; a program needn't handle non-finite values.
Results may differ from the reference program's by a relative error of at most 0.00005.
Values sent between devices are 32-bit elements; how exact they have to be, the bound alone decides.
A program may use at most 192 MiB of HBM per device.

```python
import jax
import jax.numpy as jnp
from jax import lax

CY = 32
NZ = 2048
NX = 128
NY = 512


def draw_view_sign(key, part):
    band_count = NY // CY
    order = jax.random.permutation(key, band_count)
    return (order < band_count // 2).astype(jnp.int32)


def draw_brick_flags(key, part):
    rows_y = NY // 4
    grid_shape = (NX // 8, rows_y, NZ // 128)
    dice_rolls = jax.random.randint(key, grid_shape, 0, 100)
    centre = jnp.abs(2 * jnp.arange(rows_y) - rows_y + 1)
    threshold = 95 - centre * 80 // rows_y
    return (dice_rolls < threshold[None, :, None]).astype(jnp.int32)


def steps_of(rng, shape, pieces, least, high):
    loudness, own = 1.0, jax.random.fold_in(rng, 6)
    for axis_at, shards_of in pieces:
        steps = jnp.exp(jax.random.uniform(jax.random.fold_in(own, axis_at), (shards_of,), jnp.float32, least / len(pieces), high / len(pieces)))
        loudness = loudness * jnp.repeat(steps, shape[axis_at] // shards_of).reshape([-1 if axis == axis_at else 1 for axis in range(len(shape))])
    return loudness


def scatter_about(own_key, shape, width, most, pieces=(), dtype=jnp.bfloat16):
    entries = width * jax.random.normal(own_key, shape, jnp.float32)
    if pieces:
        entries = entries * steps_of(own_key, shape, pieces, -0.22, 0.18)
    return jnp.clip(entries, -most, most).astype(dtype)


def setup_inputs(seed: int = 0) -> dict:
    arg_keys = jax.random.split(jax.random.key(seed), 4)
    velocity = scatter_about(arg_keys[0], (3, NX, NY, NZ), 1.0, 6.0, ((1, 8), (2, 16)), jnp.float32)
    view_sign = draw_view_sign(jax.random.fold_in(arg_keys[3], 71), 0)
    brick_flags = draw_brick_flags(jax.random.fold_in(arg_keys[3], 71), 0)
    return {"velocity": velocity, "view_sign": view_sign, "brick_flags": brick_flags}


ALPHA_PEAK = 0.04


def stencil(volume, along_dim):
    widths = [(0, 0)] * volume.ndim
    widths[along_dim] = (2, 2)
    padded = jnp.pad(volume, widths)
    length = volume.shape[along_dim]
    shifted = [lax.slice_in_dim(padded, k, k + length, axis=along_dim) for k in range(5)]
    return (shifted[0] - 8.0 * shifted[1] + 8.0 * shifted[3] - shifted[4]) / 12.0


def blur(volume, along_dim):
    widths = [(0, 0)] * volume.ndim
    widths[along_dim] = (1, 1)
    padded = jnp.pad(volume, widths)
    length = volume.shape[along_dim]
    return 0.25 * lax.slice_in_dim(padded, 0, length, axis=along_dim) + 0.5 * lax.slice_in_dim(padded, 1, length + 1, axis=along_dim) + 0.25 * lax.slice_in_dim(padded, 2, length + 2, axis=along_dim)


def qcriterion(gradient):
    diagonal = gradient[0][0] * gradient[0][0] + gradient[1][1] * gradient[1][1] + gradient[2][2] * gradient[2][2]
    crossed = gradient[0][1] * gradient[1][0] + gradient[0][2] * gradient[2][0] + gradient[1][2] * gradient[2][1]
    return -0.5 * (diagonal + 2.0 * crossed)


def reference(velocity, view_sign, brick_flags):
    gradient = [[stencil(velocity[i], j) for j in range(3)] for i in range(3)]
    qfield = qcriterion(gradient)
    for along_dim in range(3):
        qfield = blur(qfield, along_dim)
    speed_sq = jnp.sum(velocity * velocity, axis=0)
    flag_cells = jnp.repeat(jnp.repeat(jnp.repeat(brick_flags, 8, 0), 4, 1), 128, 2).astype(jnp.float32)
    opacity = ALPHA_PEAK * jax.nn.sigmoid(2.0 * qfield) * flag_cells
    colour = jnp.stack([jax.nn.sigmoid(qfield), jax.nn.sigmoid(speed_sq - 3.0), jax.nn.sigmoid(-2.0 * qfield)]) * opacity[None]
    flipped_rows = jnp.repeat(view_sign, CY) == 1
    opacity = jnp.where(flipped_rows[None, :, None], opacity[::-1], opacity)
    colour = jnp.where(flipped_rows[None, None, :, None], colour[:, ::-1], colour)
    transmit = jnp.cumprod(1.0 - opacity, axis=0)
    before = jnp.concatenate([jnp.ones_like(transmit[:1]), transmit[:-1]], axis=0)
    image_color = jnp.sum(before[None] * colour, axis=1)
    image_alpha = 1.0 - transmit[-1]
    return image_color, image_alpha
```

```python
import jax
import jax.numpy as jnp
from jax import lax
from jax.experimental import pallas as pl
from jax.experimental.pallas import tpu as pltpu
from jax.sharding import PartitionSpec as P

ALPHA_PEAK = 0.04
MESH = pl.DeviceIdType.MESH
LANES = 128
HALF = 8
CHUNKS = 2 * HALF


def z_gradient(row):
    even, odd = row[:, :HALF], row[:, HALF:]
    lane = lax.broadcasted_iota(jnp.int32, even.shape, 2)
    sub = lax.broadcasted_iota(jnp.int32, even.shape, 1)
    after_odd = jnp.where(sub == HALF - 1, 0.0, pltpu.roll(even, HALF - 1, 1))
    before_even = jnp.where(sub == 0, 0.0, pltpu.roll(odd, 1, 1))
    halves = []
    for mine, after, before in ((even, odd, before_even), (odd, after_odd, even)):
        near = (pltpu.roll(jnp.where(lane < 1, after, mine), LANES - 1, 2)
                - pltpu.roll(jnp.where(lane >= LANES - 1, before, mine), 1, 2))
        far = (pltpu.roll(jnp.where(lane < 2, after, mine), LANES - 2, 2)
               - pltpu.roll(jnp.where(lane >= LANES - 2, before, mine), 2, 2))
        halves.append(8.0 * near - far)
    return jnp.concatenate(halves, axis=1)


def z_blur(row):
    even, odd = row[:, :HALF], row[:, HALF:]
    lane = lax.broadcasted_iota(jnp.int32, even.shape, 2)
    sub = lax.broadcasted_iota(jnp.int32, even.shape, 1)
    after_odd = jnp.where(sub == HALF - 1, 0.0, pltpu.roll(even, HALF - 1, 1))
    before_even = jnp.where(sub == 0, 0.0, pltpu.roll(odd, 1, 1))
    halves = []
    for mine, after, before in ((even, odd, before_even), (odd, after_odd, even)):
        ahead = jnp.where(lane < 1, after, mine)
        behind = jnp.where(lane >= LANES - 1, before, mine)
        halves.append(
            (pltpu.roll(ahead, LANES - 1, 2) + pltpu.roll(behind, 1, 2)) + 2.0 * mine
        )
    return jnp.concatenate(halves, axis=1)


def q_rows(u, q, x, y, rows):
    def parts(comp):
        span = u[comp, x + 2, pl.ds(y, rows + 4)]
        near_x = u[comp, x + 3, pl.ds(y + 2, rows)] - u[comp, x + 1, pl.ds(y + 2, rows)]
        far_x = u[comp, x + 4, pl.ds(y + 2, rows)] - u[comp, x, pl.ds(y + 2, rows)]
        near_y = span[3 : rows + 3] - span[1 : rows + 1]
        far_y = span[4:] - span[:rows]
        return (
            8.0 * near_x - far_x,
            8.0 * near_y - far_y,
            z_gradient(span[2 : rows + 2]),
        )

    g00, g01, g02 = parts(0)
    total = g00 * g00
    g10, g11, g12 = parts(1)
    total = total + g11 * g11
    cross = g01 * g10
    g20, g21, g22 = parts(2)
    total = total + g22 * g22
    cross = cross + g02 * g20 + g12 * g21
    q[x + 1, pl.ds(y + 1, rows)] = total + (cross + cross)


def kernel(
    nd, nt, cx, cy, vel, sign, bricks, color, alpha,
    u, q, flags, image, pieces, load_sem,
    xs_sem, xr_sem, ys_sem, yr_sem, qs_sem, qr_sem, is_sem, ir_sem, own_sem,
):
    depth, tile = lax.axis_index("depth"), lax.axis_index("tile")
    d_next, d_prev = lax.rem(depth + 1, nd), lax.rem(depth + nd - 1, nd)
    t_next, t_prev = lax.rem(tile + 1, nt), lax.rem(tile + nt - 1, nt)
    inner = cx - 4
    mid = cy - 4

    def load(group, x0, nx, y0, ny):
        for comp in range(3):
            for chunk in range(CHUNKS):
                pltpu.make_async_copy(
                    vel.at[comp, pl.ds(x0, nx), pl.ds(y0, ny), pl.ds(chunk * LANES, LANES)],
                    u.at[comp, pl.ds(x0 + 2, nx), pl.ds(y0 + 2, ny),
                         HALF * (chunk % 2) + chunk // 2],
                    load_sem.at[group],
                ).start()

    def loaded(group, x0, nx, y0, ny):
        where = u.at[:, pl.ds(x0 + 2, nx), pl.ds(y0 + 2, ny)]
        pltpu.make_async_copy(where, where, load_sem.at[group]).wait()

    faces = ((0, cx - 2, 2, 0, cy), (1, 0, 2, 0, cy))
    edges = ((2, 2, inner, 0, 8), (3, 2, inner, cy - 8, 8))
    middle = (4, 2, inner, 8, cy - 16)
    for group in faces + edges + (middle,):
        load(*group)

    around = [(d_next, tile), (d_prev, tile), (depth, t_next), (depth, t_prev),
              (d_next, t_next), (d_next, t_prev), (d_prev, t_next), (d_prev, t_prev)]
    around += [(lax.rem(depth + hop, nd), tile) for hop in range(2, nd - 1)]
    barrier = pltpu.get_barrier_semaphore()
    for device in around:
        pl.semaphore_signal(barrier, inc=1, device_id=device, device_id_type=MESH)
    pl.semaphore_wait(barrier, len(around))

    def send(src, dst, s_sem, r_sem, device):
        copy = pltpu.make_async_remote_copy(
            src_ref=src, dst_ref=dst, send_sem=s_sem, recv_sem=r_sem,
            device_id=device, device_id_type=MESH,
        )
        copy.start()
        return copy

    bands = ((2, mid // 2), (2 + mid // 2, mid // 2), (0, 2), (cy - 2, 2))
    for group in faces:
        loaded(*group)
    x_sends = []
    for b, (y0, ny) in enumerate(bands):
        rows = pl.ds(y0 + 2, ny)
        x_sends.append((
            send(u.at[:, pl.ds(cx, 2), rows], u.at[:, pl.ds(0, 2), rows],
                 xs_sem.at[0, b], xr_sem.at[0, b], (d_next, tile)),
            send(u.at[:, pl.ds(2, 2), rows], u.at[:, pl.ds(cx + 2, 2), rows],
                 xs_sem.at[1, b], xr_sem.at[1, b], (d_prev, tile)),
        ))
    for group in edges:
        loaded(*group)
    own_x = pl.ds(2, cx)
    y_sends = (
        send(u.at[:, own_x, pl.ds(cy, 2)], u.at[:, own_x, pl.ds(0, 2)],
             ys_sem.at[0], yr_sem.at[0], (depth, t_next)),
        send(u.at[:, own_x, pl.ds(2, 2)], u.at[:, own_x, pl.ds(cy + 2, 2)],
             ys_sem.at[1], yr_sem.at[1], (depth, t_prev)),
    )
    loaded(*middle)

    position = lax.broadcasted_iota(jnp.int32, (CHUNKS, CHUNKS), 0)
    wanted = 2 * lax.rem(position, HALF) + position // HALF
    pick = lax.broadcasted_iota(jnp.int32, (CHUNKS, CHUNKS), 1) == wanted
    half_peak = 0.5 * ALPHA_PEAK
    for bx in range(cx // 8):
        rows_of = bricks[bx]
        for by in range(cy // 4):
            line = rows_of[by : by + 1].astype(jnp.float32) * half_peak
            column = jnp.sum(
                jnp.where(pick, jnp.broadcast_to(line, (CHUNKS, CHUNKS)), 0.0),
                axis=1, keepdims=True,
            )
            flags[bx, by] = jnp.broadcast_to(column, (CHUNKS, LANES))

    big = 4
    def inside(step, carry):
        q_rows(u, q, 2 + step // (mid // big), 2 + big * lax.rem(step, mid // big), big)
        return carry

    lax.fori_loop(0, inner * (mid // big), inside, 0)

    def face_x(i):
        return i + jnp.where(i >= 2, cx - 4, 0)

    q_sends = []
    for b in range(2):
        y0, ny = bands[b]
        for copy in x_sends[b]:
            copy.wait_recv()

        @pl.when(depth == 0)
        def _(y0=y0, ny=ny):
            u[:, 0:2, y0 + 2 : y0 + 2 + ny] = jnp.zeros((3, 2, ny, CHUNKS, LANES), jnp.float32)

        @pl.when(depth == nd - 1)
        def _(y0=y0, ny=ny):
            u[:, cx + 2 : cx + 4, y0 + 2 : y0 + 2 + ny] = jnp.zeros(
                (3, 2, ny, CHUNKS, LANES), jnp.float32)

        def outside(step, carry, y0=y0, ny=ny):
            q_rows(u, q, face_x(step // (ny // 2)), y0 + 2 * lax.rem(step, ny // 2), 2)
            return carry

        lax.fori_loop(0, 4 * (ny // 2), outside, 0)
        rows = pl.ds(y0 + 1, ny)
        q_sends.append(send(q.at[cx, rows], q.at[0, rows],
                            qs_sem.at[len(q_sends)], qr_sem.at[len(q_sends)], (d_next, tile)))
        q_sends.append(send(q.at[1, rows], q.at[cx + 1, rows],
                            qs_sem.at[len(q_sends)], qr_sem.at[len(q_sends)], (d_prev, tile)))

    for b in (2, 3):
        for copy in x_sends[b]:
            copy.wait_recv()
    for copy in y_sends:
        copy.wait_recv()

    for b in (2, 3):
        y0 = bands[b][0]

        @pl.when(depth == 0)
        def _(y0=y0):
            u[:, 0:2, y0 + 2 : y0 + 4] = jnp.zeros((3, 2, 2, CHUNKS, LANES), jnp.float32)

        @pl.when(depth == nd - 1)
        def _(y0=y0):
            u[:, cx + 2 : cx + 4, y0 + 2 : y0 + 4] = jnp.zeros((3, 2, 2, CHUNKS, LANES), jnp.float32)

    @pl.when(tile == 0)
    def _():
        u[:, 2 : cx + 2, 0:2] = jnp.zeros((3, cx, 2, CHUNKS, LANES), jnp.float32)

    @pl.when(tile == nt - 1)
    def _():
        u[:, 2 : cx + 2, cy + 2 : cy + 4] = jnp.zeros((3, cx, 2, CHUNKS, LANES), jnp.float32)

    def rim(step, carry):
        q_rows(u, q, step // 2, (cy - 2) * lax.rem(step, 2), 2)
        return carry

    lax.fori_loop(0, 2 * cx, rim, 0)
    own_q = pl.ds(1, cx)
    last = (
        (q.at[own_q, cy], q.at[own_q, 0], (depth, t_next)),
        (q.at[own_q, 1], q.at[own_q, cy + 1], (depth, t_prev)),
        (q.at[cx, pl.ds(1, 2)], q.at[0, pl.ds(1, 2)], (d_next, tile)),
        (q.at[1, pl.ds(1, 2)], q.at[cx + 1, pl.ds(1, 2)], (d_prev, tile)),
        (q.at[cx, pl.ds(cy - 1, 2)], q.at[0, pl.ds(cy - 1, 2)], (d_next, tile)),
        (q.at[1, pl.ds(cy - 1, 2)], q.at[cx + 1, pl.ds(cy - 1, 2)], (d_prev, tile)),
        (q.at[cx, cy], q.at[0, 0], (d_next, t_next)),
        (q.at[cx, 1], q.at[0, cy + 1], (d_next, t_prev)),
        (q.at[1, cy], q.at[cx + 1, 0], (d_prev, t_next)),
        (q.at[1, 1], q.at[cx + 1, cy + 1], (d_prev, t_prev)),
    )
    for src, dst, device in last:
        k = len(q_sends)
        q_sends.append(send(src, dst, qs_sem.at[k], qr_sem.at[k], device))
    for copy in q_sends:
        copy.wait_recv()

    @pl.when(depth == 0)
    def _():
        q[0] = jnp.zeros((cy + 2, CHUNKS, LANES), jnp.float32)

    @pl.when(depth == nd - 1)
    def _():
        q[cx + 1] = jnp.zeros((cy + 2, CHUNKS, LANES), jnp.float32)

    @pl.when(tile == 0)
    def _():
        q[:, 0] = jnp.zeros((cx + 2, CHUNKS, LANES), jnp.float32)

    @pl.when(tile == nt - 1)
    def _():
        q[:, cy + 1] = jnp.zeros((cx + 2, CHUNKS, LANES), jnp.float32)

    flip = sign[0]
    scale = -1.0 / (288.0 * 64.0)

    def rows_pair(pair, carry):
        y = 2 * pair

        def along(view):
            return view + flip * (cx - 1 - 2 * view)

        def y_blurred(x):
            span = q[x + 1, pl.ds(y, 4)]
            return (span[0:2] + span[2:4]) + 2.0 * span[1:3]

        def layer(view, state):
            before, here, trans, sum_a, sum_b, sum_c = state
            x = along(view)
            after = y_blurred(along(view + 1))
            smooth = z_blur((before + after) + 2.0 * here)
            v0 = u[0, x + 2, pl.ds(y + 2, 2)]
            v1 = u[1, x + 2, pl.ds(y + 2, 2)]
            v2 = u[2, x + 2, pl.ds(y + 2, 2)]
            speed = v0 * v0 + v1 * v1 + v2 * v2
            peak = flags[x // 8, y // 4][None]
            tanh_q = jnp.tanh(scale * smooth)
            tanh_half = jnp.tanh((0.5 * scale) * smooth)
            tanh_speed = jnp.tanh(0.5 * speed - 1.5)
            weight = trans * (peak + peak * tanh_q)
            return (here, after, trans - weight, sum_a + weight * tanh_half,
                    sum_b + weight * tanh_speed, sum_c + weight * tanh_q)

        one = jnp.ones((2, CHUNKS, LANES), jnp.float32)
        zero = jnp.zeros((2, CHUNKS, LANES), jnp.float32)
        state = (y_blurred(along(-1)), y_blurred(along(0)), one, zero, zero, zero)
        state = lax.fori_loop(0, cx, layer, state, unroll=2)
        _, _, trans, sum_a, sum_b, sum_c = state
        covered = 1.0 - trans
        rows = pl.ds(y, 2)
        image[0, rows] = trans
        image[1, rows] = 0.5 * (covered + sum_a)
        image[2, rows] = 0.5 * (covered + sum_b)
        image[3, rows] = 0.5 * (covered - sum_c)
        return carry

    lax.fori_loop(0, cy // 2, rows_pair, 0)

    def piece(d, par, where):
        return image.at[:, :, HALF * par + d], pieces.at[where, :, :, pl.ds(par * LANES, LANES)]

    for d in range(nd):
        for par in range(2):
            src, dst = piece(d, par, depth)

            @pl.when(depth != d)
            def _(src=src, dst=dst, d=d, par=par):
                send(src, dst, is_sem.at[d, par], ir_sem.at[depth, par], (d, tile))

            @pl.when(depth == d)
            def _(src=src, dst=dst, par=par):
                pltpu.make_async_copy(src, dst, own_sem.at[par]).start()

    for d in range(nd):
        for par in range(2):
            src, dst = piece(d, par, d)

            @pl.when(depth != d)
            def _(src=src, dst=dst, d=d, par=par):
                copy = pltpu.make_async_remote_copy(
                    src_ref=src, dst_ref=dst, send_sem=is_sem.at[d, par],
                    recv_sem=ir_sem.at[d, par], device_id=(d, tile), device_id_type=MESH)
                copy.wait()

            @pl.when(depth == d)
            def _(src=src, dst=dst, par=par):
                pltpu.make_async_copy(src, dst, own_sem.at[par]).wait()

    total = None
    for view in range(nd):
        part = pieces[view + flip * (nd - 1 - 2 * view)]
        if total is None:
            trans, shade = part[0], part[1:]
        else:
            shade = shade + trans[None] * part[1:]
            trans = trans * part[0]
        total = view
    color[...] = shade
    alpha[...] = 1.0 - trans

    for pair in x_sends:
        for copy in pair:
            copy.wait_send()
    for copy in y_sends:
        copy.wait_send()
    for copy in q_sends:
        copy.wait_send()


def solution(mesh):
    nd, nt = mesh.shape["depth"], mesh.shape["tile"]

    def per_device(velocity, view_sign, brick_flags):
        _, cx, cy, cz = velocity.shape
        width = cz // nd
        dma = pltpu.SemaphoreType.DMA

        def body(*refs):
            kernel(nd, nt, cx, cy, *refs)

        return pl.pallas_call(
            body,
            out_shape=(
                jax.ShapeDtypeStruct((3, cy, width), jnp.float32),
                jax.ShapeDtypeStruct((cy, width), jnp.float32),
            ),
            in_specs=[
                pl.BlockSpec(memory_space=pl.ANY),
                pl.BlockSpec(memory_space=pltpu.SMEM),
                pl.BlockSpec(memory_space=pltpu.VMEM),
            ],
            out_specs=(
                pl.BlockSpec(memory_space=pltpu.VMEM),
                pl.BlockSpec(memory_space=pltpu.VMEM),
            ),
            scratch_shapes=[
                pltpu.VMEM((3, cx + 4, cy + 4, CHUNKS, LANES), jnp.float32),
                pltpu.VMEM((cx + 2, cy + 2, CHUNKS, LANES), jnp.float32),
                pltpu.VMEM((cx // 8, cy // 4, CHUNKS, LANES), jnp.float32),
                pltpu.VMEM((4, cy, CHUNKS, LANES), jnp.float32),
                pltpu.VMEM((nd, 4, cy, width), jnp.float32),
                dma((5,)),
                dma((2, 4)), dma((2, 4)), dma((2,)), dma((2,)),
                dma((14,)), dma((14,)), dma((nd, 2)), dma((nd, 2)), dma((2,)),
            ],
            compiler_params=pltpu.CompilerParams(
                collective_id=0, has_side_effects=True, vmem_limit_bytes=56 << 20
            ),
        )(velocity, view_sign, brick_flags)

    placed = (P(None, "depth", "tile", None), P("tile"), P("depth", "tile", None))
    return jax.shard_map(
        per_device,
        mesh=mesh,
        in_specs=placed,
        out_specs=(P(None, "tile", "depth"), P("tile", "depth")),
        check_vma=False,
    )
```

```python
import jax
import jax.numpy as jnp
from jax import lax
from jax.experimental import pallas as pl
from jax.experimental.pallas import tpu as pltpu
from jax.sharding import PartitionSpec as P

ALPHA_PEAK = 0.04
MESH = pl.DeviceIdType.MESH
LANES = 128
HALF = 8
CHUNKS = 2 * HALF


def split(value):
    high = value.astype(jnp.bfloat16)
    return high, (value - high.astype(jnp.float32)).astype(jnp.bfloat16)


def band_matrix(taps):
    shape = (6 * LANES, 2 * LANES)
    row = lax.broadcasted_iota(jnp.int32, shape, 0)
    lane = lax.rem(row, LANES)
    apart = jnp.where(lane < LANES // 2, lane + 2 * LANES, lane - LANES)
    cell = jnp.where(row < 4 * LANES, lax.rem(row, 2 * LANES), apart)
    offset = cell - lax.broadcasted_iota(jnp.int32, shape, 1)
    band = jnp.zeros(shape, jnp.float32)
    for at, weight in taps:
        band = jnp.where(offset == at, weight, band)
    return band.astype(jnp.bfloat16)


def along_z(value, band):
    lead = value.shape[:-2]
    flat = value.reshape((-1, CHUNKS, LANES))
    even, odd = flat[:, :HALF], flat[:, HALF:]
    lane = lax.broadcasted_iota(jnp.int32, even.shape, 2)
    sub = lax.broadcasted_iota(jnp.int32, even.shape, 1)
    beside = jnp.where(lane < 2, pltpu.roll(even, HALF - 1, 1), pltpu.roll(odd, 1, 1))
    outside = ((lane < 2) & (sub == HALF - 1)) | ((lane >= 2) & (sub == 0))
    beside = jnp.where(outside, 0.0, beside)
    parts = [split(v.reshape((-1, LANES))) for v in (even, odd, beside)]
    (e_hi, e_lo), (o_hi, o_lo), (b_hi, b_lo) = parts
    operand = jnp.concatenate([e_hi, o_hi, e_lo, o_lo, b_hi, b_lo], axis=1)
    out = jnp.dot(operand, band[...], preferred_element_type=jnp.float32)
    halves = [out[:, h * LANES : (h + 1) * LANES].reshape((-1, HALF, LANES)) for h in range(2)]
    return jnp.concatenate(halves, axis=1).reshape(lead + (CHUNKS, LANES))


def q_rows(u, gz, q, x, y, rows):
    def parts(comp):
        span = u[comp, x + 2, pl.ds(y, rows + 4)]
        near_x = u[comp, x + 3, pl.ds(y + 2, rows)] - u[comp, x + 1, pl.ds(y + 2, rows)]
        far_x = u[comp, x + 4, pl.ds(y + 2, rows)] - u[comp, x, pl.ds(y + 2, rows)]
        near_y = span[3 : rows + 3] - span[1 : rows + 1]
        far_y = span[4:] - span[:rows]
        return (
            8.0 * near_x - far_x,
            8.0 * near_y - far_y,
            gz[comp, x, pl.ds(y, rows)],
        )

    g00, g01, g02 = parts(0)
    total = g00 * g00
    g10, g11, g12 = parts(1)
    total = total + g11 * g11
    cross = g01 * g10
    g20, g21, g22 = parts(2)
    total = total + g22 * g22
    cross = cross + g02 * g20 + g12 * g21
    q[x, pl.ds(y, rows)] = total + (cross + cross)


def kernel(
    nd, nt, cx, cy, vel, sign, bricks, color, alpha,
    u, gz, raw, q, q_low, q_high, slope, smoother, flags, image, pieces, load_sem,
    xs_sem, xr_sem, ys_sem, yr_sem, qs_sem, qr_sem, is_sem, ir_sem, own_sem,
):
    depth, tile = lax.axis_index("depth"), lax.axis_index("tile")
    d_next, d_prev = lax.rem(depth + 1, nd), lax.rem(depth + nd - 1, nd)
    t_next, t_prev = lax.rem(tile + 1, nt), lax.rem(tile + nt - 1, nt)
    inner = cx - 4
    mid = cy - 4

    def load(group, x0, nx, y0, ny):
        for comp in range(3):
            for chunk in range(CHUNKS):
                pltpu.make_async_copy(
                    vel.at[comp, pl.ds(x0, nx), pl.ds(y0, ny), pl.ds(chunk * LANES, LANES)],
                    u.at[comp, pl.ds(x0 + 2, nx), pl.ds(y0 + 2, ny),
                         HALF * (chunk % 2) + chunk // 2],
                    load_sem.at[group],
                ).start()

    def loaded(group, x0, nx, y0, ny):
        where = u.at[:, pl.ds(x0 + 2, nx), pl.ds(y0 + 2, ny)]
        pltpu.make_async_copy(where, where, load_sem.at[group]).wait()

    faces = ((0, cx - 2, 2, 0, cy), (1, 0, 2, 0, cy))
    edges = ((2, 2, inner, 0, 8), (3, 2, inner, cy - 8, 8))
    middle = (4, 2, inner, 8, cy - 16)
    for group in faces + edges + (middle,):
        load(*group)

    around = [(d_next, tile), (d_prev, tile), (depth, t_next), (depth, t_prev),
              (d_next, t_next), (d_next, t_prev), (d_prev, t_next), (d_prev, t_prev)]
    around += [(lax.rem(depth + hop, nd), tile) for hop in range(2, nd - 1)]
    barrier = pltpu.get_barrier_semaphore()
    for device in around:
        pl.semaphore_signal(barrier, inc=1, device_id=device, device_id_type=MESH)
    pl.semaphore_wait(barrier, len(around))

    def send(src, dst, s_sem, r_sem, device):
        copy = pltpu.make_async_remote_copy(
            src_ref=src, dst_ref=dst, send_sem=s_sem, recv_sem=r_sem,
            device_id=device, device_id_type=MESH,
        )
        copy.start()
        return copy

    first = mid // 8 * 4
    bands = ((2, first), (2 + first, mid - first), (0, 2), (cy - 2, 2))
    for group in faces:
        loaded(*group)
    x_sends = []
    for b, (y0, ny) in enumerate(bands):
        rows = pl.ds(y0 + 2, ny)
        x_sends.append((
            send(u.at[:, pl.ds(cx, 2), rows], u.at[:, pl.ds(0, 2), rows],
                 xs_sem.at[0, b], xr_sem.at[0, b], (d_next, tile)),
            send(u.at[:, pl.ds(2, 2), rows], u.at[:, pl.ds(cx + 2, 2), rows],
                 xs_sem.at[1, b], xr_sem.at[1, b], (d_prev, tile)),
        ))
    for group in edges:
        loaded(*group)
    own_x = pl.ds(2, cx)
    y_sends = (
        send(u.at[:, own_x, pl.ds(cy, 2)], u.at[:, own_x, pl.ds(0, 2)],
             ys_sem.at[0], yr_sem.at[0], (depth, t_next)),
        send(u.at[:, own_x, pl.ds(2, 2)], u.at[:, own_x, pl.ds(cy + 2, 2)],
             ys_sem.at[1], yr_sem.at[1], (depth, t_prev)),
    )
    loaded(*middle)

    position = lax.broadcasted_iota(jnp.int32, (CHUNKS, CHUNKS), 0)
    wanted = 2 * lax.rem(position, HALF) + position // HALF
    pick = lax.broadcasted_iota(jnp.int32, (CHUNKS, CHUNKS), 1) == wanted
    half_peak = 0.5 * ALPHA_PEAK
    for bx in range(cx // 8):
        rows_of = bricks[bx]
        for by in range(cy // 4):
            line = rows_of[by : by + 1].astype(jnp.float32) * half_peak
            column = jnp.sum(
                jnp.where(pick, jnp.broadcast_to(line, (CHUNKS, CHUNKS)), 0.0),
                axis=1, keepdims=True,
            )
            flags[bx, by] = jnp.broadcast_to(column, (CHUNKS, LANES))

    slope[...] = band_matrix(((-2, 1.0), (-1, -8.0), (1, 8.0), (2, -1.0)))
    smoother[...] = band_matrix(((-1, 1.0), (0, 2.0), (1, 1.0)))
    own_y = pl.ds(2, cy)

    def z_plane(x, carry):
        for comp in range(3):
            gz[comp, x] = along_z(u[comp, x + 2, own_y], slope)
        return carry

    lax.fori_loop(0, cx, z_plane, 0)

    big = 4

    def inside(step, carry):
        x = step + 2

        def block(k, carry):
            q_rows(u, gz, raw, x, 2 + big * k, big)
            return carry

        lax.fori_loop(0, mid // big, block, 0)
        q[x + 1] = along_z(raw[x, pl.ds(2, mid)], smoother)
        return carry

    lax.fori_loop(0, inner, inside, 0)

    def face_x(i):
        return i + jnp.where(i >= 2, cx - 4, 0)

    q_sends = []

    def send_q(src, dst, device):
        k = len(q_sends)
        q_sends.append(send(src, dst, qs_sem.at[k], qr_sem.at[k], device))

    for b in range(2):
        y0, ny = bands[b]
        for copy in x_sends[b]:
            copy.wait_recv()

        @pl.when(depth == 0)
        def _(y0=y0, ny=ny):
            u[:, 0:2, y0 + 2 : y0 + 2 + ny] = jnp.zeros((3, 2, ny, CHUNKS, LANES), jnp.float32)

        @pl.when(depth == nd - 1)
        def _(y0=y0, ny=ny):
            u[:, cx + 2 : cx + 4, y0 + 2 : y0 + 2 + ny] = jnp.zeros(
                (3, 2, ny, CHUNKS, LANES), jnp.float32)

        def outside(step, carry, y0=y0, ny=ny):
            q_rows(u, gz, raw, face_x(step // (ny // big)), y0 + big * lax.rem(step, ny // big), big)
            return carry

        lax.fori_loop(0, 4 * (ny // big), outside, 0)
        rows = pl.ds(y0 - 2, ny)
        for x0 in (0, cx - 2):
            q[pl.ds(x0 + 1, 2), rows] = along_z(raw[pl.ds(x0, 2), pl.ds(y0, ny)], smoother)
        send_q(q.at[cx, rows], q.at[0, rows], (d_next, tile))
        send_q(q.at[1, rows], q.at[cx + 1, rows], (d_prev, tile))

    for b in (2, 3):
        for copy in x_sends[b]:
            copy.wait_recv()
    for copy in y_sends:
        copy.wait_recv()

    for b in (2, 3):
        y0 = bands[b][0]

        @pl.when(depth == 0)
        def _(y0=y0):
            u[:, 0:2, y0 + 2 : y0 + 4] = jnp.zeros((3, 2, 2, CHUNKS, LANES), jnp.float32)

        @pl.when(depth == nd - 1)
        def _(y0=y0):
            u[:, cx + 2 : cx + 4, y0 + 2 : y0 + 4] = jnp.zeros((3, 2, 2, CHUNKS, LANES), jnp.float32)

    @pl.when(tile == 0)
    def _():
        u[:, 2 : cx + 2, 0:2] = jnp.zeros((3, cx, 2, CHUNKS, LANES), jnp.float32)

    @pl.when(tile == nt - 1)
    def _():
        u[:, 2 : cx + 2, cy + 2 : cy + 4] = jnp.zeros((3, cx, 2, CHUNKS, LANES), jnp.float32)

    def rim(x, carry):
        q_rows(u, gz, raw, x, 0, 2)
        q_rows(u, gz, raw, x, cy - 2, 2)
        return carry

    lax.fori_loop(0, cx, rim, 0)
    own_q = pl.ds(1, cx)
    q_low[own_q, 1:3] = along_z(raw[:, 0:2], smoother)
    q_high[own_q, 0:2] = along_z(raw[:, cy - 2 : cy], smoother)
    inner_sends = len(q_sends)
    send_q(q_high.at[own_q, 1], q_low.at[own_q, 0], (depth, t_next))
    send_q(q_low.at[own_q, 1], q_high.at[own_q, 2], (depth, t_prev))
    for part, rows in ((q_low, pl.ds(1, 2)), (q_high, pl.ds(0, 2))):
        send_q(part.at[cx, rows], part.at[0, rows], (d_next, tile))
        send_q(part.at[1, rows], part.at[cx + 1, rows], (d_prev, tile))
    send_q(q_high.at[cx, 1], q_low.at[0, 0], (d_next, t_next))
    send_q(q_low.at[cx, 1], q_high.at[0, 2], (d_next, t_prev))
    send_q(q_high.at[1, 1], q_low.at[cx + 1, 0], (d_prev, t_next))
    send_q(q_low.at[1, 1], q_high.at[cx + 1, 2], (d_prev, t_prev))

    for copy in q_sends[:inner_sends]:
        copy.wait_recv()

    @pl.when(depth == 0)
    def _():
        q[0] = jnp.zeros((mid, CHUNKS, LANES), jnp.float32)

    @pl.when(depth == nd - 1)
    def _():
        q[cx + 1] = jnp.zeros((mid, CHUNKS, LANES), jnp.float32)

    flip = sign[0]
    scale = -1.0 / (288.0 * 64.0)

    def along(view):
        return view + flip * (cx - 1 - 2 * view)

    def composite(y, rows, span_of, unroll):
        def y_blurred(x):
            span = span_of(x)
            return (span[0:rows] + span[2 : rows + 2]) + 2.0 * span[1 : rows + 1]

        def layer(view, state):
            before, here, trans, sum_a, sum_b, sum_c = state
            x = along(view)
            after = y_blurred(along(view + 1))
            smooth = (before + after) + 2.0 * here
            v0 = u[0, x + 2, pl.ds(y + 2, rows)]
            v1 = u[1, x + 2, pl.ds(y + 2, rows)]
            v2 = u[2, x + 2, pl.ds(y + 2, rows)]
            speed = v0 * v0 + v1 * v1 + v2 * v2
            peak = flags[x // 8, y // 4][None]
            tanh_q = jnp.tanh(scale * smooth)
            tanh_half = jnp.tanh((0.5 * scale) * smooth)
            tanh_speed = jnp.tanh(0.5 * speed - 1.5)
            weight = trans * (peak + peak * tanh_q)
            return (here, after, trans - weight, sum_a + weight * tanh_half,
                    sum_b + weight * tanh_speed, sum_c + weight * tanh_q)

        one = jnp.ones((rows, CHUNKS, LANES), jnp.float32)
        zero = jnp.zeros((rows, CHUNKS, LANES), jnp.float32)
        state = (y_blurred(along(-1)), y_blurred(along(0)), one, zero, zero, zero)
        state = lax.fori_loop(0, cx, layer, state, unroll=unroll)
        _, _, trans, sum_a, sum_b, sum_c = state
        covered = 1.0 - trans
        where = pl.ds(y, rows)
        image[0, where] = trans
        image[1, where] = 0.5 * (covered + sum_a)
        image[2, where] = 0.5 * (covered + sum_b)
        image[3, where] = 0.5 * (covered - sum_c)

    def middle_rows(y0, count):
        def pair(k, carry):
            y = y0 + 2 * k
            composite(y, 2, lambda x: q[x + 1, pl.ds(y - 3, 4)], 4)
            return carry

        lax.fori_loop(0, count // 2, pair, 0)

    def piece(d, par, where, group):
        rows = pl.ds(8 * group, 8)
        return image.at[:, rows, HALF * par + d], pieces.at[where, :, par, rows]

    def send_image(group):
        for hop in range(1, nd):
            for d in range(nd):
                @pl.when(d == lax.rem(depth + hop, nd))
                def _(d=d):
                    for par in range(2):
                        src, dst = piece(d, par, depth, group)
                        send(src, dst, is_sem.at[group, d, par], ir_sem.at[group, depth, par], (d, tile))
        for d in range(nd):
            @pl.when(depth == d)
            def _(d=d):
                for par in range(2):
                    src, dst = piece(d, par, depth, group)
                    pltpu.make_async_copy(src, dst, own_sem.at[group, par]).start()

    groups = cy // 8
    for group in range(1, groups - 1):
        middle_rows(8 * group, 8)
        send_image(group)
    middle_rows(4, 4)
    middle_rows(cy - 8, 4)

    for copy in q_sends[inner_sends:]:
        copy.wait_recv()

    @pl.when(depth == 0)
    def _():
        q_low[0] = jnp.zeros((3, CHUNKS, LANES), jnp.float32)
        q_high[0] = jnp.zeros((3, CHUNKS, LANES), jnp.float32)

    @pl.when(depth == nd - 1)
    def _():
        q_low[cx + 1] = jnp.zeros((3, CHUNKS, LANES), jnp.float32)
        q_high[cx + 1] = jnp.zeros((3, CHUNKS, LANES), jnp.float32)

    @pl.when(tile == 0)
    def _():
        q_low[:, 0] = jnp.zeros((cx + 2, CHUNKS, LANES), jnp.float32)

    @pl.when(tile == nt - 1)
    def _():
        q_high[:, 2] = jnp.zeros((cx + 2, CHUNKS, LANES), jnp.float32)

    composite(0, 4, lambda x: jnp.concatenate([q_low[x + 1], q[x + 1, 0:3]], axis=0), 2)
    send_image(0)
    composite(cy - 4, 4, lambda x: jnp.concatenate(
        [q[x + 1, mid - 3 : mid], q_high[x + 1]], axis=0), 2)
    send_image(groups - 1)

    for group in list(range(1, groups - 1)) + [0, groups - 1]:
        for d in range(nd):
            @pl.when(depth != d)
            def _(d=d, group=group):
                for par in range(2):
                    src, _ = piece(d, par, depth, group)
                    _, dst = piece(d, par, d, group)
                    pltpu.make_async_remote_copy(
                        src_ref=src, dst_ref=dst, send_sem=is_sem.at[group, d, par],
                        recv_sem=ir_sem.at[group, d, par], device_id=(d, tile),
                        device_id_type=MESH).wait()

            @pl.when(depth == d)
            def _(d=d, group=group):
                for par in range(2):
                    src, dst = piece(d, par, d, group)
                    pltpu.make_async_copy(src, dst, own_sem.at[group, par]).wait()

    total = None
    for view in range(nd):
        part = pieces[view + flip * (nd - 1 - 2 * view)]
        if total is None:
            trans, shade = part[0], part[1:]
        else:
            shade = shade + trans[None] * part[1:]
            trans = trans * part[0]
        total = view
    for par in range(2):
        lanes = slice(par * LANES, (par + 1) * LANES)
        color[:, :, lanes] = shade[:, par]
        alpha[:, lanes] = 1.0 - trans[par]

    for pair in x_sends:
        for copy in pair:
            copy.wait_send()
    for copy in y_sends:
        copy.wait_send()
    for copy in q_sends:
        copy.wait_send()


def solution(mesh):
    nd, nt = mesh.shape["depth"], mesh.shape["tile"]

    def per_device(velocity, view_sign, brick_flags):
        _, cx, cy, cz = velocity.shape
        width = cz // nd
        dma = pltpu.SemaphoreType.DMA

        def body(*refs):
            kernel(nd, nt, cx, cy, *refs)

        return pl.pallas_call(
            body,
            out_shape=(
                jax.ShapeDtypeStruct((3, cy, width), jnp.float32),
                jax.ShapeDtypeStruct((cy, width), jnp.float32),
            ),
            in_specs=[
                pl.BlockSpec(memory_space=pl.ANY),
                pl.BlockSpec(memory_space=pltpu.SMEM),
                pl.BlockSpec(memory_space=pltpu.VMEM),
            ],
            out_specs=(
                pl.BlockSpec(memory_space=pltpu.VMEM),
                pl.BlockSpec(memory_space=pltpu.VMEM),
            ),
            scratch_shapes=[
                pltpu.VMEM((3, cx + 4, cy + 4, CHUNKS, LANES), jnp.float32),
                pltpu.VMEM((3, cx, cy, CHUNKS, LANES), jnp.float32),
                pltpu.VMEM((cx, cy, CHUNKS, LANES), jnp.float32),
                pltpu.VMEM((cx + 2, cy - 4, CHUNKS, LANES), jnp.float32),
                pltpu.VMEM((cx + 2, 3, CHUNKS, LANES), jnp.float32),
                pltpu.VMEM((cx + 2, 3, CHUNKS, LANES), jnp.float32),
                pltpu.VMEM((6 * LANES, 2 * LANES), jnp.bfloat16),
                pltpu.VMEM((6 * LANES, 2 * LANES), jnp.bfloat16),
                pltpu.VMEM((cx // 8, cy // 4, CHUNKS, LANES), jnp.float32),
                pltpu.VMEM((4, cy, CHUNKS, LANES), jnp.float32),
                pltpu.VMEM((nd, 4, 2, cy, width // 2), jnp.float32),
                dma((5,)),
                dma((2, 4)), dma((2, 4)), dma((2,)), dma((2,)),
                dma((14,)), dma((14,)), dma((cy // 8, nd, 2)), dma((cy // 8, nd, 2)), dma((cy // 8, 2)),
            ],
            compiler_params=pltpu.CompilerParams(
                collective_id=0, has_side_effects=True, vmem_limit_bytes=56 << 20
            ),
        )(velocity, view_sign, brick_flags)

    placed = (P(None, "depth", "tile", None), P("tile"), P("depth", "tile", None))
    return jax.shard_map(
        per_device,
        mesh=mesh,
        in_specs=placed,
        out_specs=(P(None, "tile", "depth"), P("tile", "depth")),
        check_vma=False,
    )
```

```python
import jax
import jax.numpy as jnp
from jax import lax
from jax.experimental import pallas as pl
from jax.experimental.pallas import tpu as pltpu
from jax.sharding import PartitionSpec as P

ALPHA_PEAK = 0.04
MESH = pl.DeviceIdType.MESH
LANES = 128
HALF = 8
CHUNKS = 2 * HALF


def split(value):
    high = value.astype(jnp.bfloat16)
    return high, (value - high.astype(jnp.float32)).astype(jnp.bfloat16)


def band_matrix(taps):
    shape = (6 * LANES, 2 * LANES)
    row = lax.broadcasted_iota(jnp.int32, shape, 0)
    lane = lax.rem(row, LANES)
    apart = jnp.where(lane < LANES // 2, lane + 2 * LANES, lane - LANES)
    cell = jnp.where(row < 4 * LANES, lax.rem(row, 2 * LANES), apart)
    offset = cell - lax.broadcasted_iota(jnp.int32, shape, 1)
    band = jnp.zeros(shape, jnp.float32)
    for at, weight in taps:
        band = jnp.where(offset == at, weight, band)
    return band.astype(jnp.bfloat16)


def along_z(value, band):
    lead = value.shape[:-2]
    flat = value.reshape((-1, CHUNKS, LANES))
    even, odd = flat[:, :HALF], flat[:, HALF:]
    lane = lax.broadcasted_iota(jnp.int32, even.shape, 2)
    sub = lax.broadcasted_iota(jnp.int32, even.shape, 1)
    beside = jnp.where(lane < 2, pltpu.roll(even, HALF - 1, 1), pltpu.roll(odd, 1, 1))
    outside = ((lane < 2) & (sub == HALF - 1)) | ((lane >= 2) & (sub == 0))
    beside = jnp.where(outside, 0.0, beside)
    parts = [split(v.reshape((-1, LANES))) for v in (even, odd, beside)]
    (e_hi, e_lo), (o_hi, o_lo), (b_hi, b_lo) = parts
    operand = jnp.concatenate([e_hi, o_hi, e_lo, o_lo, b_hi, b_lo], axis=1)
    out = jnp.dot(operand, band[...], preferred_element_type=jnp.float32)
    halves = [out[:, h * LANES : (h + 1) * LANES].reshape((-1, HALF, LANES)) for h in range(2)]
    return jnp.concatenate(halves, axis=1).reshape(lead + (CHUNKS, LANES))


def q_rows(u, gz, q, x, y, rows):
    def parts(comp):
        span = u[comp, x + 2, pl.ds(y, rows + 4)]
        near_x = u[comp, x + 3, pl.ds(y + 2, rows)] - u[comp, x + 1, pl.ds(y + 2, rows)]
        far_x = u[comp, x + 4, pl.ds(y + 2, rows)] - u[comp, x, pl.ds(y + 2, rows)]
        near_y = span[3 : rows + 3] - span[1 : rows + 1]
        far_y = span[4:] - span[:rows]
        return (
            8.0 * near_x - far_x,
            8.0 * near_y - far_y,
            gz[comp, x, pl.ds(y, rows)],
        )

    g00, g01, g02 = parts(0)
    total = g00 * g00
    g10, g11, g12 = parts(1)
    total = total + g11 * g11
    cross = g01 * g10
    g20, g21, g22 = parts(2)
    total = total + g22 * g22
    cross = cross + g02 * g20 + g12 * g21
    q[x, pl.ds(y, rows)] = total + (cross + cross)


def kernel(
    nd, nt, cx, cy, vel, sign, bricks, result,
    u, gz, raw, q, q_low, q_high, slope, smoother, flags, image, near, merged, far, load_sem,
    xs_sem, xr_sem, ys_sem, yr_sem, qs_sem, qr_sem, is_sem, ir_sem, own_sem, fs_sem, fr_sem,
):
    depth, tile = lax.axis_index("depth"), lax.axis_index("tile")
    d_next, d_prev = lax.rem(depth + 1, nd), lax.rem(depth + nd - 1, nd)
    t_next, t_prev = lax.rem(tile + 1, nt), lax.rem(tile + nt - 1, nt)
    inner = cx - 4
    mid = cy - 4

    def load(group, x0, nx, y0, ny):
        for comp in range(3):
            for chunk in range(CHUNKS):
                pltpu.make_async_copy(
                    vel.at[comp, pl.ds(x0, nx), pl.ds(y0, ny), pl.ds(chunk * LANES, LANES)],
                    u.at[comp, pl.ds(x0 + 2, nx), pl.ds(y0 + 2, ny),
                         HALF * (chunk % 2) + chunk // 2],
                    load_sem.at[group],
                ).start()

    def loaded(group, x0, nx, y0, ny):
        where = u.at[:, pl.ds(x0 + 2, nx), pl.ds(y0 + 2, ny)]
        pltpu.make_async_copy(where, where, load_sem.at[group]).wait()

    faces = ((0, cx - 2, 2, 0, cy), (1, 0, 2, 0, cy))
    edges = ((2, 2, inner, 0, 8), (3, 2, inner, cy - 8, 8))
    middle = (4, 2, inner, 8, cy - 16)
    for group in faces + edges + (middle,):
        load(*group)

    around = [(d_next, tile), (d_prev, tile), (depth, t_next), (depth, t_prev),
              (d_next, t_next), (d_next, t_prev), (d_prev, t_next), (d_prev, t_prev)]
    around += [(lax.rem(depth + hop, nd), tile) for hop in range(2, nd, 2)]
    barrier = pltpu.get_barrier_semaphore()
    for device in around:
        pl.semaphore_signal(barrier, inc=1, device_id=device, device_id_type=MESH)
    pl.semaphore_wait(barrier, len(around))

    def send(src, dst, s_sem, r_sem, device):
        copy = pltpu.make_async_remote_copy(
            src_ref=src, dst_ref=dst, send_sem=s_sem, recv_sem=r_sem,
            device_id=device, device_id_type=MESH,
        )
        copy.start()
        return copy

    bands = ((10, cy - 20), (0, 2), (cy - 2, 2), (2, 8), (cy - 10, 8))
    for group in faces:
        loaded(*group)
    x_sends, y_sends = {}, {}

    def issue_x(b):
        y0, ny = bands[b]
        rows = pl.ds(y0 + 2, ny)
        x_sends[b] = (
            send(u.at[:, pl.ds(cx, 2), rows], u.at[:, pl.ds(0, 2), rows],
                 xs_sem.at[0, b], xr_sem.at[0, b], (d_next, tile)),
            send(u.at[:, pl.ds(2, 2), rows], u.at[:, pl.ds(cx + 2, 2), rows],
                 xs_sem.at[1, b], xr_sem.at[1, b], (d_prev, tile)),
        )

    half = cx // 2

    def issue_y(h):
        part_x = pl.ds(2 + h * half, half)
        y_sends[h] = (
            send(u.at[:, part_x, pl.ds(cy, 2)], u.at[:, part_x, pl.ds(0, 2)],
                 ys_sem.at[0, h], yr_sem.at[0, h], (depth, t_next)),
            send(u.at[:, part_x, pl.ds(2, 2)], u.at[:, part_x, pl.ds(cy + 2, 2)],
                 ys_sem.at[1, h], yr_sem.at[1, h], (depth, t_prev)),
        )

    issue_x(0)
    issue_x(3)
    for group in edges:
        loaded(*group)
    issue_y(0)
    loaded(*middle)

    position = lax.broadcasted_iota(jnp.int32, (CHUNKS, CHUNKS), 0)
    wanted = 2 * lax.rem(position, HALF) + position // HALF
    pick = lax.broadcasted_iota(jnp.int32, (CHUNKS, CHUNKS), 1) == wanted
    half_peak = 0.5 * ALPHA_PEAK
    for bx in range(cx // 8):
        rows_of = bricks[bx]
        for by in range(cy // 4):
            line = rows_of[by : by + 1].astype(jnp.float32) * half_peak
            column = jnp.sum(
                jnp.where(pick, jnp.broadcast_to(line, (CHUNKS, CHUNKS)), 0.0),
                axis=1, keepdims=True,
            )
            flags[bx, by] = jnp.broadcast_to(column, (CHUNKS, LANES))

    slope[...] = band_matrix(((-2, 1.0), (-1, -8.0), (1, 8.0), (2, -1.0)))
    smoother[...] = band_matrix(((-1, 1.0), (0, 2.0), (1, 1.0)))
    own_y = pl.ds(2, cy)

    def z_plane(x, carry):
        for comp in range(3):
            gz[comp, x] = along_z(u[comp, x + 2, own_y], slope)
        return carry

    lax.fori_loop(0, cx, z_plane, 0)
    for b in (1, 2, 4):
        issue_x(b)
    issue_y(1)

    big = 4

    def inside(step, carry):
        x = step + 2

        def block(k, carry):
            q_rows(u, gz, raw, x, 2 + big * k, big)
            return carry

        lax.fori_loop(0, mid // big, block, 0)
        q[x + 1] = along_z(raw[x, pl.ds(2, mid)], smoother)
        return carry

    def face_x(i):
        return i + jnp.where(i >= 2, cx - 4, 0)

    q_sends, rim_sends = [], []

    def send_q(src, dst, device, into):
        k = len(q_sends) + len(rim_sends)
        into.append(send(src, dst, qs_sem.at[k], qr_sem.at[k], device))

    def x_arrived(b):
        y0, ny = bands[b]
        for copy in x_sends[b]:
            copy.wait_recv()

        @pl.when(depth == 0)
        def _():
            u[:, 0:2, y0 + 2 : y0 + 2 + ny] = jnp.zeros((3, 2, ny, CHUNKS, LANES), jnp.float32)

        @pl.when(depth == nd - 1)
        def _():
            u[:, cx + 2 : cx + 4, y0 + 2 : y0 + 2 + ny] = jnp.zeros(
                (3, 2, ny, CHUNKS, LANES), jnp.float32)

    def outside(b):
        y0, ny = bands[b]

        def block(step, carry):
            q_rows(u, gz, raw, face_x(step // (ny // big)), y0 + big * lax.rem(step, ny // big), big)
            return carry

        lax.fori_loop(0, 4 * (ny // big), block, 0)
        rows = pl.ds(y0 - 2, ny)
        for x0 in (0, cx - 2):
            q[pl.ds(x0 + 1, 2), rows] = along_z(raw[pl.ds(x0, 2), pl.ds(y0, ny)], smoother)
        send_q(q.at[cx, rows], q.at[0, rows], (d_next, tile), q_sends)
        send_q(q.at[1, rows], q.at[cx + 1, rows], (d_prev, tile), q_sends)

    def rim(h):
        for copy in y_sends[h]:
            copy.wait_recv()

        @pl.when(tile == 0)
        def _():
            u[:, 2 + h * half : 2 + h * half + half, 0:2] = jnp.zeros(
                (3, half, 2, CHUNKS, LANES), jnp.float32)

        @pl.when(tile == nt - 1)
        def _():
            u[:, 2 + h * half : 2 + h * half + half, cy + 2 : cy + 4] = jnp.zeros(
                (3, half, 2, CHUNKS, LANES), jnp.float32)

        def both(x, carry):
            q_rows(u, gz, raw, x, 0, 2)
            q_rows(u, gz, raw, x, cy - 2, 2)
            return carry

        lax.fori_loop(h * half, h * half + half, both, 0)
        own_q, own_raw = pl.ds(1 + h * half, half), pl.ds(h * half, half)
        q_low[own_q, 1:3] = along_z(raw[own_raw, 0:2], smoother)
        q_high[own_q, 0:2] = along_z(raw[own_raw, cy - 2 : cy], smoother)
        send_q(q_high.at[own_q, 1], q_low.at[own_q, 0], (depth, t_next), rim_sends)
        send_q(q_low.at[own_q, 1], q_high.at[own_q, 2], (depth, t_prev), rim_sends)
        at, to, device = (1, cx + 1, d_prev) if h == 0 else (cx, 0, d_next)
        send_q(q_low.at[at, pl.ds(1, 2)], q_low.at[to, pl.ds(1, 2)], (device, tile), rim_sends)
        send_q(q_high.at[at, pl.ds(0, 2)], q_high.at[to, pl.ds(0, 2)], (device, tile), rim_sends)
        send_q(q_high.at[at, 1], q_low.at[to, 0], (device, t_next), rim_sends)
        send_q(q_low.at[at, 1], q_high.at[to, 2], (device, t_prev), rim_sends)

    lax.fori_loop(0, inner // 2, inside, 0)
    for b in (0, 3):
        x_arrived(b)
        outside(b)
    lax.fori_loop(inner // 2, inner, inside, 0)
    for b in (1, 2, 4):
        x_arrived(b)
    outside(4)
    rim(0)
    rim(1)

    for copy in q_sends:
        copy.wait_recv()

    @pl.when(depth == 0)
    def _():
        q[0] = jnp.zeros((mid, CHUNKS, LANES), jnp.float32)

    @pl.when(depth == nd - 1)
    def _():
        q[cx + 1] = jnp.zeros((mid, CHUNKS, LANES), jnp.float32)

    flip = sign[0]
    scale = -1.0 / (288.0 * 64.0)

    def along(view):
        return view + flip * (cx - 1 - 2 * view)

    def image_row(y):
        if isinstance(y, int):
            return y - 4 if 4 <= y < cy - 4 else (y + cy - 8 if y < 4 else y)
        return y - 4

    def composite(y, rows, span_of, unroll):
        def y_blurred(x):
            span = span_of(x)
            return (span[0:rows] + span[2 : rows + 2]) + 2.0 * span[1 : rows + 1]

        def layer(view, state):
            before, here, trans, sum_a, sum_b, sum_c = state
            x = along(view)
            after = y_blurred(along(view + 1))
            smooth = (before + after) + 2.0 * here
            v0 = u[0, x + 2, pl.ds(y + 2, rows)]
            v1 = u[1, x + 2, pl.ds(y + 2, rows)]
            v2 = u[2, x + 2, pl.ds(y + 2, rows)]
            speed = v0 * v0 + v1 * v1 + v2 * v2
            peak = flags[x // 8, y // 4][None]
            tanh_q = jnp.tanh(scale * smooth)
            tanh_half = jnp.tanh((0.5 * scale) * smooth)
            tanh_speed = jnp.tanh(0.5 * speed - 1.5)
            weight = trans * (peak + peak * tanh_q)
            return (here, after, trans - weight, sum_a + weight * tanh_half,
                    sum_b + weight * tanh_speed, sum_c + weight * tanh_q)

        one = jnp.ones((rows, CHUNKS, LANES), jnp.float32)
        zero = jnp.zeros((rows, CHUNKS, LANES), jnp.float32)
        state = (y_blurred(along(-1)), y_blurred(along(0)), one, zero, zero, zero)
        state = lax.fori_loop(0, cx, layer, state, unroll=unroll)
        _, _, trans, sum_a, sum_b, sum_c = state
        covered = 1.0 - trans
        where = pl.ds(image_row(y), rows)
        image[0, where] = trans
        image[1, where] = 0.5 * (covered + sum_a)
        image[2, where] = 0.5 * (covered + sum_b)
        image[3, where] = 0.5 * (covered - sum_c)

    def middle_rows(y0, count):
        def pair(k, carry):
            y = y0 + 2 * k
            composite(y, 2, lambda x: q[x + 1, pl.ds(y - 3, 4)], 4)
            return carry

        lax.fori_loop(0, count // 2, pair, 0)

    chip, core = depth // 2, lax.rem(depth, 2)
    chips = nd // 2

    def near_copies(group, core_at):
        rows = pl.ds(8 * group, 8)
        give, keep = [], []
        for to in range(chips):
            for par in range(2):
                k = 2 * to + par
                dst = near.at[core_at, to, :, par, rows]
                src = image.at[:, rows, HALF * par + 2 * to + (1 - core_at)]
                give.append(pltpu.make_async_remote_copy(
                    src_ref=src, dst_ref=dst, send_sem=is_sem.at[group, k],
                    recv_sem=ir_sem.at[group, k], device_id=(2 * chip + (1 - core_at), tile),
                    device_id_type=MESH))
                src = image.at[:, rows, HALF * par + 2 * to + core_at]
                keep.append(pltpu.make_async_copy(src, dst, own_sem.at[group, k]))
        return give, keep

    def send_near(group):
        for core_at in range(2):
            @pl.when(core == core_at)
            def _(core_at=core_at):
                for copies in near_copies(group, core_at):
                    for copy in copies:
                        copy.start()

    def far_copy(group, to, source):
        rows = pl.ds(8 * group, 8)
        return pltpu.make_async_remote_copy(
            src_ref=merged.at[to, :, :, rows], dst_ref=far.at[source, :, :, rows],
            send_sem=fs_sem.at[group, to], recv_sem=fr_sem.at[group, source],
            device_id=(2 * to + core, tile), device_id_type=MESH)

    def merge_near(group):
        for core_at in range(2):
            @pl.when(core == core_at)
            def _(core_at=core_at):
                for copies in near_copies(group, core_at):
                    for copy in copies:
                        copy.wait()
        rows = pl.ds(8 * group, 8)
        straight = flip == 0
        for to in range(chips):
            one, two = near[0, to, :, :, rows], near[1, to, :, :, rows]
            front, back = jnp.where(straight, one, two), jnp.where(straight, two, one)
            trans = front[0] * back[0]
            shade = front[1:] + front[0][None] * back[1:]
            merged[to, 0, :, rows] = trans
            merged[to, 1:4, :, rows] = shade

            @pl.when(chip == to)
            def _(to=to, trans=trans, shade=shade):
                far[to, 0, :, rows] = trans
                far[to, 1:4, :, rows] = shade
        for to in range(chips):
            @pl.when(chip != to)
            def _(to=to):
                far_copy(group, to, chip).start()

    middle_rows(4, 8)
    send_near(0)
    middle_rows(12, 8)
    send_near(1)
    merge_near(0)
    middle_rows(20, 8)
    send_near(2)
    merge_near(1)

    for copy in rim_sends:
        copy.wait_recv()

    @pl.when(depth == 0)
    def _():
        q_low[0] = jnp.zeros((3, CHUNKS, LANES), jnp.float32)
        q_high[0] = jnp.zeros((3, CHUNKS, LANES), jnp.float32)

    @pl.when(depth == nd - 1)
    def _():
        q_low[cx + 1] = jnp.zeros((3, CHUNKS, LANES), jnp.float32)
        q_high[cx + 1] = jnp.zeros((3, CHUNKS, LANES), jnp.float32)

    @pl.when(tile == 0)
    def _():
        q_low[:, 0] = jnp.zeros((cx + 2, CHUNKS, LANES), jnp.float32)

    @pl.when(tile == nt - 1)
    def _():
        q_high[:, 2] = jnp.zeros((cx + 2, CHUNKS, LANES), jnp.float32)

    composite(0, 4, lambda x: jnp.concatenate([q_low[x + 1], q[x + 1, 0:3]], axis=0), 2)
    composite(cy - 4, 4, lambda x: jnp.concatenate(
        [q[x + 1, mid - 3 : mid], q_high[x + 1]], axis=0), 2)
    send_near(3)
    merge_near(2)
    merge_near(3)

    for group in range(4):
        for to in range(chips):
            @pl.when(chip != to)
            def _(group=group, to=to):
                far_copy(group, to, to).wait()

    trans = shade = None
    for view in range(chips):
        part = far[view + flip * (chips - 1 - 2 * view)]
        if trans is None:
            trans, shade = part[0], part[1:]
        else:
            shade = shade + trans[None] * part[1:]
            trans = trans * part[0]
    for par in range(2):
        lanes = slice(par * LANES, (par + 1) * LANES)
        for y0, at, ny in ((4, 0, cy - 8), (0, cy - 8, 4), (cy - 4, cy - 4, 4)):
            result[1:4, y0 : y0 + ny, lanes] = shade[:, par, at : at + ny]
            result[0, y0 : y0 + ny, lanes] = 1.0 - trans[par, at : at + ny]

    for pair in list(x_sends.values()) + list(y_sends.values()):
        for copy in pair:
            copy.wait_send()
    for copy in q_sends + rim_sends:
        copy.wait_send()


def solution(mesh):
    nd, nt = mesh.shape["depth"], mesh.shape["tile"]

    def per_device(velocity, view_sign, brick_flags):
        _, cx, cy, cz = velocity.shape
        width = cz // nd
        dma = pltpu.SemaphoreType.DMA

        def body(*refs):
            kernel(nd, nt, cx, cy, *refs)

        result = pl.pallas_call(
            body,
            out_shape=jax.ShapeDtypeStruct((4, cy, width), jnp.float32),
            in_specs=[
                pl.BlockSpec(memory_space=pl.ANY),
                pl.BlockSpec(memory_space=pltpu.SMEM),
                pl.BlockSpec(memory_space=pltpu.VMEM),
            ],
            out_specs=pl.BlockSpec(memory_space=pltpu.VMEM),
            scratch_shapes=[
                pltpu.VMEM((3, cx + 4, cy + 4, CHUNKS, LANES), jnp.float32),
                pltpu.VMEM((3, cx, cy, CHUNKS, LANES), jnp.float32),
                pltpu.VMEM((cx, cy, CHUNKS, LANES), jnp.float32),
                pltpu.VMEM((cx + 2, cy - 4, CHUNKS, LANES), jnp.float32),
                pltpu.VMEM((cx + 2, 3, CHUNKS, LANES), jnp.float32),
                pltpu.VMEM((cx + 2, 3, CHUNKS, LANES), jnp.float32),
                pltpu.VMEM((6 * LANES, 2 * LANES), jnp.bfloat16),
                pltpu.VMEM((6 * LANES, 2 * LANES), jnp.bfloat16),
                pltpu.VMEM((cx // 8, cy // 4, CHUNKS, LANES), jnp.float32),
                pltpu.VMEM((4, cy, CHUNKS, LANES), jnp.float32),
                pltpu.VMEM((2, nd // 2, 4, 2, cy, LANES), jnp.float32),
                pltpu.VMEM((nd // 2, 4, 2, cy, LANES), jnp.float32),
                pltpu.VMEM((nd // 2, 4, 2, cy, LANES), jnp.float32),
                dma((5,)),
                dma((2, 5)), dma((2, 5)), dma((2, 2)), dma((2, 2)),
                dma((18,)), dma((18,)), dma((cy // 8, nd)), dma((cy // 8, nd)), dma((cy // 8, nd)),
                dma((cy // 8, nd // 2)), dma((cy // 8, nd // 2)),
            ],
            compiler_params=pltpu.CompilerParams(
                collective_id=0, has_side_effects=True, vmem_limit_bytes=56 << 20
            ),
        )(velocity, view_sign, brick_flags)

        def hand_over(result_ref, color_ref, alpha_ref):
            color_ref[...] = result_ref[1:4]
            alpha_ref[...] = result_ref[0]

        return pl.pallas_call(
            hand_over,
            out_shape=(
                jax.ShapeDtypeStruct((3, cy, width), jnp.float32),
                jax.ShapeDtypeStruct((cy, width), jnp.float32),
            ),
        )(result)

    placed = (P(None, "depth", "tile", None), P("tile"), P("depth", "tile", None))
    return jax.shard_map(
        per_device,
        mesh=mesh,
        in_specs=placed,
        out_specs=(P(None, "tile", "depth"), P("tile", "depth")),
        check_vma=False,
    )
```

```python
import jax
import jax.numpy as jnp
from jax import lax
from jax.experimental import pallas as pl
from jax.experimental.pallas import tpu as pltpu
from jax.sharding import PartitionSpec as P

ALPHA_PEAK = 0.04
MESH = pl.DeviceIdType.MESH
LANES = 128
HALF = 8
CHUNKS = 2 * HALF


def split(value):
    high = value.astype(jnp.bfloat16)
    return high, (value - high.astype(jnp.float32)).astype(jnp.bfloat16)


def band_matrix(taps):
    shape = (6 * LANES, 2 * LANES)
    row = lax.broadcasted_iota(jnp.int32, shape, 0)
    lane = lax.rem(row, LANES)
    apart = jnp.where(lane < LANES // 2, lane + 2 * LANES, lane - LANES)
    cell = jnp.where(row < 4 * LANES, lax.rem(row, 2 * LANES), apart)
    offset = cell - lax.broadcasted_iota(jnp.int32, shape, 1)
    band = jnp.zeros(shape, jnp.float32)
    for at, weight in taps:
        band = jnp.where(offset == at, weight, band)
    return band.astype(jnp.bfloat16)


def along_z(value, band):
    lead = value.shape[:-2]
    flat = value.reshape((-1, CHUNKS, LANES))
    even, odd = flat[:, :HALF], flat[:, HALF:]
    lane = lax.broadcasted_iota(jnp.int32, even.shape, 2)
    sub = lax.broadcasted_iota(jnp.int32, even.shape, 1)
    beside = jnp.where(lane < 2, pltpu.roll(even, HALF - 1, 1), pltpu.roll(odd, 1, 1))
    outside = ((lane < 2) & (sub == HALF - 1)) | ((lane >= 2) & (sub == 0))
    beside = jnp.where(outside, 0.0, beside)
    parts = [split(v.reshape((-1, LANES))) for v in (even, odd, beside)]
    (e_hi, e_lo), (o_hi, o_lo), (b_hi, b_lo) = parts
    operand = jnp.concatenate([e_hi, o_hi, e_lo, o_lo, b_hi, b_lo], axis=1)
    out = jnp.dot(operand, band[...], preferred_element_type=jnp.float32)
    halves = [out[:, h * LANES : (h + 1) * LANES].reshape((-1, HALF, LANES)) for h in range(2)]
    return jnp.concatenate(halves, axis=1).reshape(lead + (CHUNKS, LANES))


def q_rows(u, gz, q, x, y, rows):
    def parts(comp):
        span = u[comp, x + 2, pl.ds(y, rows + 4)]
        near_x = u[comp, x + 3, pl.ds(y + 2, rows)] - u[comp, x + 1, pl.ds(y + 2, rows)]
        far_x = u[comp, x + 4, pl.ds(y + 2, rows)] - u[comp, x, pl.ds(y + 2, rows)]
        near_y = span[3 : rows + 3] - span[1 : rows + 1]
        far_y = span[4:] - span[:rows]
        return (
            8.0 * near_x - far_x,
            8.0 * near_y - far_y,
            gz[comp, x, pl.ds(y, rows)],
        )

    g00, g01, g02 = parts(0)
    total = g00 * g00
    g10, g11, g12 = parts(1)
    total = total + g11 * g11
    cross = g01 * g10
    g20, g21, g22 = parts(2)
    total = total + g22 * g22
    cross = cross + g02 * g20 + g12 * g21
    q[x, pl.ds(y, rows)] = total + (cross + cross)


def kernel(
    nd, nt, cx, cy, vel, sign, bricks, result,
    u, gz, glow, raw, q, face_a, face_b, q_low, q_high, slope, smoother, flags, image, near, merged, far, load_sem,
    xs_sem, xr_sem, ys_sem, yr_sem, qs_sem, qr_sem, is_sem, ir_sem, own_sem, fs_sem, fr_sem,
):
    depth, tile = lax.axis_index("depth"), lax.axis_index("tile")
    d_next, d_prev = lax.rem(depth + 1, nd), lax.rem(depth + nd - 1, nd)
    t_next, t_prev = lax.rem(tile + 1, nt), lax.rem(tile + nt - 1, nt)
    inner = cx - 4
    mid = cy - 4

    def load(group, x0, nx, y0, ny):
        for comp in range(3):
            for chunk in range(CHUNKS):
                pltpu.make_async_copy(
                    vel.at[comp, pl.ds(x0, nx), pl.ds(y0, ny), pl.ds(chunk * LANES, LANES)],
                    u.at[comp, pl.ds(x0 + 2, nx), pl.ds(y0 + 2, ny),
                         HALF * (chunk % 2) + chunk // 2],
                    load_sem.at[group],
                ).start()

    def loaded(group, x0, nx, y0, ny):
        where = u.at[:, pl.ds(x0 + 2, nx), pl.ds(y0 + 2, ny)]
        pltpu.make_async_copy(where, where, load_sem.at[group]).wait()

    faces = ((0, cx - 2, 2, 0, cy), (1, 0, 2, 0, cy))
    edges = ((2, 2, inner, 0, 8), (3, 2, inner, cy - 8, 8))
    middle = (4, 2, inner, 8, cy - 16)
    around = [(d_next, tile), (d_prev, tile), (depth, t_next), (depth, t_prev),
              (d_next, t_next), (d_next, t_prev), (d_prev, t_next), (d_prev, t_prev)]
    around += [(lax.rem(depth + hop, nd), tile) for hop in range(2, nd, 2)]
    barrier = pltpu.get_barrier_semaphore()
    for device in around:
        pl.semaphore_signal(barrier, inc=1, device_id=device, device_id_type=MESH)
    for group in faces + edges + (middle,):
        load(*group)
    pl.semaphore_wait(barrier, len(around))

    def send(src, dst, s_sem, r_sem, device):
        copy = pltpu.make_async_remote_copy(
            src_ref=src, dst_ref=dst, send_sem=s_sem, recv_sem=r_sem,
            device_id=device, device_id_type=MESH,
        )
        copy.start()
        return copy

    bands = ((2, cy - 12), (0, 2), (cy - 2, 2), (cy - 10, 8))
    for group in faces:
        loaded(*group)
    x_sends, y_sends = {}, {}

    def issue_x(b):
        y0, ny = bands[b]
        rows = pl.ds(y0 + 2, ny)
        x_sends[b] = (
            send(u.at[:, pl.ds(cx, 2), rows], u.at[:, pl.ds(0, 2), rows],
                 xs_sem.at[0, b], xr_sem.at[0, b], (d_next, tile)),
            send(u.at[:, pl.ds(2, 2), rows], u.at[:, pl.ds(cx + 2, 2), rows],
                 xs_sem.at[1, b], xr_sem.at[1, b], (d_prev, tile)),
        )

    half = cx // 2

    def issue_y(h):
        part_x = pl.ds(2 + h * half, half)
        y_sends[h] = (
            send(u.at[:, part_x, pl.ds(cy, 2)], u.at[:, part_x, pl.ds(0, 2)],
                 ys_sem.at[0, h], yr_sem.at[0, h], (depth, t_next)),
            send(u.at[:, part_x, pl.ds(2, 2)], u.at[:, part_x, pl.ds(cy + 2, 2)],
                 ys_sem.at[1, h], yr_sem.at[1, h], (depth, t_prev)),
        )

    for b in (0, 1, 2):
        issue_x(b)
    for group in edges:
        loaded(*group)
    issue_y(0)
    loaded(*middle)

    position = lax.broadcasted_iota(jnp.int32, (CHUNKS, CHUNKS), 0)
    wanted = 2 * lax.rem(position, HALF) + position // HALF
    pick = lax.broadcasted_iota(jnp.int32, (CHUNKS, CHUNKS), 1) == wanted
    half_peak = 0.5 * ALPHA_PEAK
    for bx in range(cx // 8):
        rows_of = bricks[bx]
        for by in range(cy // 4):
            line = rows_of[by : by + 1].astype(jnp.float32) * half_peak
            column = jnp.sum(
                jnp.where(pick, jnp.broadcast_to(line, (CHUNKS, CHUNKS)), 0.0),
                axis=1, keepdims=True,
            )
            flags[bx, by] = jnp.broadcast_to(column, (CHUNKS, LANES))

    slope[...] = band_matrix(((-2, 1.0), (-1, -8.0), (1, 8.0), (2, -1.0)))
    smoother[...] = band_matrix(((-1, 1.0), (0, 2.0), (1, 1.0)))
    own_y = pl.ds(2, cy)

    def z_plane(x, carry):
        for comp in range(3):
            gz[comp, x] = along_z(u[comp, x + 2, own_y], slope)
        return carry

    lax.fori_loop(0, cx, z_plane, 0)
    issue_x(3)
    issue_y(1)

    def glow_plane(x, carry):
        def speed(k, carry):
            rows = pl.ds(4 * k, 4)
            squares = [u[comp, x + 2, pl.ds(4 * k + 2, 4)] for comp in range(3)]
            squares = [v * v for v in squares]
            glow[x, rows] = jnp.tanh(0.5 * (squares[0] + squares[1] + squares[2]) - 1.5)
            return carry

        return lax.fori_loop(0, cy // 4, speed, carry)

    lax.fori_loop(0, cx, glow_plane, 0)
    big = 4

    def inside(step, carry):
        x = step + 2

        def block(k, carry):
            q_rows(u, gz, raw, x, 2 + big * k, big)
            return carry

        lax.fori_loop(0, mid // big, block, 0)
        q[x] = along_z(raw[x, pl.ds(2, mid)], smoother)
        return carry

    def face_x(i):
        return i + jnp.where(i >= 2, cx - 4, 0)

    q_sends, rim_sends = [], []

    def send_q(src, dst, device, into):
        k = len(q_sends) + len(rim_sends)
        into.append(send(src, dst, qs_sem.at[k], qr_sem.at[k], device))

    def x_arrived(b):
        y0, ny = bands[b]
        for copy in x_sends[b]:
            copy.wait_recv()

        @pl.when(depth == 0)
        def _():
            u[:, 0:2, y0 + 2 : y0 + 2 + ny] = jnp.zeros((3, 2, ny, CHUNKS, LANES), jnp.float32)

        @pl.when(depth == nd - 1)
        def _():
            u[:, cx + 2 : cx + 4, y0 + 2 : y0 + 2 + ny] = jnp.zeros(
                (3, 2, ny, CHUNKS, LANES), jnp.float32)

    def outside(b):
        y0, ny = bands[b]

        def block(step, carry):
            q_rows(u, gz, raw, face_x(step // (ny // big)), y0 + big * lax.rem(step, ny // big), big)
            return carry

        lax.fori_loop(0, 4 * (ny // big), block, 0)
        rows = pl.ds(y0 - 2, ny)
        for x0 in (0, cx - 2):
            q[pl.ds(x0, 2), rows] = along_z(raw[pl.ds(x0, 2), pl.ds(y0, ny)], smoother)
        face = face_a if b == 0 else face_b
        send_q(q.at[cx - 1, rows], face.at[0], (d_next, tile), q_sends)
        send_q(q.at[0, rows], face.at[1], (d_prev, tile), q_sends)

    def rim(h):
        for copy in y_sends[h]:
            copy.wait_recv()

        @pl.when(tile == 0)
        def _():
            u[:, 2 + h * half : 2 + h * half + half, 0:2] = jnp.zeros(
                (3, half, 2, CHUNKS, LANES), jnp.float32)

        @pl.when(tile == nt - 1)
        def _():
            u[:, 2 + h * half : 2 + h * half + half, cy + 2 : cy + 4] = jnp.zeros(
                (3, half, 2, CHUNKS, LANES), jnp.float32)

        def both(x, carry):
            q_rows(u, gz, raw, x, 0, 2)
            q_rows(u, gz, raw, x, cy - 2, 2)
            return carry

        lax.fori_loop(h * half, h * half + half, both, 0)
        own_q, own_raw = pl.ds(1 + h * half, half), pl.ds(h * half, half)
        q_low[own_q, 1:3] = along_z(raw[own_raw, 0:2], smoother)
        q_high[own_q, 0:2] = along_z(raw[own_raw, cy - 2 : cy], smoother)
        send_q(q_high.at[own_q, 1], q_low.at[own_q, 0], (depth, t_next), rim_sends)
        send_q(q_low.at[own_q, 1], q_high.at[own_q, 2], (depth, t_prev), rim_sends)
        at, to, device = (1, cx + 1, d_prev) if h == 0 else (cx, 0, d_next)
        send_q(q_low.at[at, pl.ds(1, 2)], q_low.at[to, pl.ds(1, 2)], (device, tile), rim_sends)
        send_q(q_high.at[at, pl.ds(0, 2)], q_high.at[to, pl.ds(0, 2)], (device, tile), rim_sends)
        send_q(q_high.at[at, 1], q_low.at[to, 0], (device, t_next), rim_sends)
        send_q(q_low.at[at, 1], q_high.at[to, 2], (device, t_prev), rim_sends)

    flip = sign[0]
    scale = -1.0 / (288.0 * 64.0)

    def along(view):
        return view + flip * (cx - 1 - 2 * view)

    def image_row(y):
        if isinstance(y, int):
            return y - 4 if 4 <= y < cy - 4 else (y + cy - 8 if y < 4 else y)
        return y - 4

    def composite(y, rows, span_of, unroll):
        def y_blurred(x, face=False):
            span = span_of(x, face)
            return (span[0:rows] + span[2 : rows + 2]) + 2.0 * span[1 : rows + 1]

        def shade_layer(x, after, state):
            before, here, trans, sum_a, sum_b, sum_c = state
            smooth = (before + after) + 2.0 * here
            peak = flags[x // 8, y // 4][None]
            tanh_q = jnp.tanh(scale * smooth)
            tanh_half = jnp.tanh((0.5 * scale) * smooth)
            tanh_speed = glow[x, pl.ds(y, rows)]
            weight = trans * (peak + peak * tanh_q)
            return (here, after, trans - weight, sum_a + weight * tanh_half,
                    sum_b + weight * tanh_speed, sum_c + weight * tanh_q)

        def layer(view, state):
            return shade_layer(along(view), y_blurred(along(view + 1)), state)

        one = jnp.ones((rows, CHUNKS, LANES), jnp.float32)
        zero = jnp.zeros((rows, CHUNKS, LANES), jnp.float32)
        state = (y_blurred(flip, True), y_blurred(along(0)), one, zero, zero, zero)
        state = lax.fori_loop(0, cx - 1, layer, state, unroll=unroll)
        state = shade_layer(along(cx - 1), y_blurred(1 - flip, True), state)
        _, _, trans, sum_a, sum_b, sum_c = state
        covered = 1.0 - trans
        where = pl.ds(image_row(y), rows)
        image[0, where] = trans
        image[1, where] = 0.5 * (covered + sum_a)
        image[2, where] = 0.5 * (covered + sum_b)
        image[3, where] = 0.5 * (covered - sum_c)

    def span_a(y):
        return lambda x, face: (face_a if face else q)[x, pl.ds(y - 3, 4)]

    def span_b(y):
        return lambda x, face: face_b[x, pl.ds(y - cy + 9, 4)] if face else q[x, pl.ds(y - 3, 4)]

    def span_ab(y):
        cut = cy - 10 - (y - 1)

        def span(x, face):
            if not face:
                return q[x, y - 3 : y + 1]
            return jnp.concatenate([face_a[x, y - 3 : y - 3 + cut], face_b[x, 0 : 4 - cut]], axis=0)

        return span

    def span_low(x, face):
        if face:
            return jnp.concatenate([q_low[x * (cx + 1)], face_a[x, 0:3]], axis=0)
        return jnp.concatenate([q_low[x + 1], q[x, 0:3]], axis=0)

    def span_high(x, face):
        if face:
            return jnp.concatenate([face_b[x, 5:8], q_high[x * (cx + 1)]], axis=0)
        return jnp.concatenate([q[x, mid - 3 : mid], q_high[x + 1]], axis=0)

    def row_pairs(y0, count, span):
        def pair(k, carry):
            y = y0 + 2 * k
            composite(y, 2, span(y), 5)
            return carry

        lax.fori_loop(0, count // 2, pair, 0)

    chip, core = depth // 2, lax.rem(depth, 2)
    chips = nd // 2

    def near_copies(group, core_at):
        rows = pl.ds(8 * group, 8)
        give, keep = [], []
        for to in range(chips):
            for par in range(2):
                k = 2 * to + par
                dst = near.at[core_at, to, :, par, rows]
                src = image.at[:, rows, HALF * par + 2 * to + (1 - core_at)]
                give.append(pltpu.make_async_remote_copy(
                    src_ref=src, dst_ref=dst, send_sem=is_sem.at[group, k],
                    recv_sem=ir_sem.at[group, k], device_id=(2 * chip + (1 - core_at), tile),
                    device_id_type=MESH))
                src = image.at[:, rows, HALF * par + 2 * to + core_at]
                keep.append(pltpu.make_async_copy(src, dst, own_sem.at[group, k]))
        return give, keep

    def send_near(group):
        for core_at in range(2):
            @pl.when(core == core_at)
            def _(core_at=core_at):
                for copies in near_copies(group, core_at):
                    for copy in copies:
                        copy.start()

    def far_copy(group, to, source):
        rows = pl.ds(8 * group, 8)
        return pltpu.make_async_remote_copy(
            src_ref=merged.at[to, :, :, rows], dst_ref=far.at[source, :, :, rows],
            send_sem=fs_sem.at[group, to], recv_sem=fr_sem.at[group, source],
            device_id=(2 * to + core, tile), device_id_type=MESH)

    def merge_near(group):
        for core_at in range(2):
            @pl.when(core == core_at)
            def _(core_at=core_at):
                for copies in near_copies(group, core_at):
                    for copy in copies:
                        copy.wait()
        rows = pl.ds(8 * group, 8)
        straight = flip == 0
        for to in range(chips):
            one, two = near[0, to, :, :, rows], near[1, to, :, :, rows]
            front, back = jnp.where(straight, one, two), jnp.where(straight, two, one)
            trans = front[0] * back[0]
            shade = front[1:] + front[0][None] * back[1:]
            merged[to, 0, :, rows] = trans
            merged[to, 1:4, :, rows] = shade

            @pl.when(chip == to)
            def _(to=to, trans=trans, shade=shade):
                far[to, 0, :, rows] = trans
                far[to, 1:4, :, rows] = shade
        for to in range(chips):
            @pl.when(chip != to)
            def _(to=to):
                far_copy(group, to, chip).start()

    def faces_arrived(copies, face):
        for copy in copies:
            copy.wait_recv()

        @pl.when(depth == 0)
        def _():
            face[0] = jnp.zeros(face.shape[1:], jnp.float32)

        @pl.when(depth == nd - 1)
        def _():
            face[1] = jnp.zeros(face.shape[1:], jnp.float32)

    lax.fori_loop(0, inner // 2, inside, 0)
    x_arrived(0)
    outside(0)
    x_arrived(1)
    x_arrived(2)
    rim(0)
    lax.fori_loop(inner // 2, inner, inside, 0)
    rim(1)
    x_arrived(3)
    outside(3)
    faces_arrived(q_sends[:2], face_a)
    row_pairs(4, 8, span_a)
    send_near(0)
    row_pairs(12, 8, span_a)
    send_near(1)
    merge_near(0)
    faces_arrived(q_sends[2:], face_b)
    composite(cy - 12, 2, span_ab(cy - 12), 5)
    composite(cy - 10, 2, span_ab(cy - 10), 5)
    row_pairs(cy - 8, 4, span_b)
    send_near(2)
    merge_near(1)

    for copy in rim_sends:
        copy.wait_recv()

    @pl.when(depth == 0)
    def _():
        q_low[0] = jnp.zeros((3, CHUNKS, LANES), jnp.float32)
        q_high[0] = jnp.zeros((3, CHUNKS, LANES), jnp.float32)

    @pl.when(depth == nd - 1)
    def _():
        q_low[cx + 1] = jnp.zeros((3, CHUNKS, LANES), jnp.float32)
        q_high[cx + 1] = jnp.zeros((3, CHUNKS, LANES), jnp.float32)

    @pl.when(tile == 0)
    def _():
        q_low[:, 0] = jnp.zeros((cx + 2, CHUNKS, LANES), jnp.float32)

    @pl.when(tile == nt - 1)
    def _():
        q_high[:, 2] = jnp.zeros((cx + 2, CHUNKS, LANES), jnp.float32)

    composite(0, 4, span_low, 3)
    composite(cy - 4, 4, span_high, 3)
    send_near(3)
    merge_near(2)
    merge_near(3)

    for group in range(4):
        for to in range(chips):
            @pl.when(chip != to)
            def _(group=group, to=to):
                far_copy(group, to, to).wait()

    trans = shade = None
    for view in range(chips):
        part = far[view + flip * (chips - 1 - 2 * view)]
        if trans is None:
            trans, shade = part[0], part[1:]
        else:
            shade = shade + trans[None] * part[1:]
            trans = trans * part[0]
    for par in range(2):
        lanes = slice(par * LANES, (par + 1) * LANES)
        for y0, at, ny in ((4, 0, cy - 8), (0, cy - 8, 4), (cy - 4, cy - 4, 4)):
            result[1:4, y0 : y0 + ny, lanes] = shade[:, par, at : at + ny]
            result[0, y0 : y0 + ny, lanes] = 1.0 - trans[par, at : at + ny]

    for pair in list(x_sends.values()) + list(y_sends.values()):
        for copy in pair:
            copy.wait_send()
    for copy in q_sends + rim_sends:
        copy.wait_send()


def solution(mesh):
    nd, nt = mesh.shape["depth"], mesh.shape["tile"]

    def per_device(velocity, view_sign, brick_flags):
        _, cx, cy, cz = velocity.shape
        width = cz // nd
        dma = pltpu.SemaphoreType.DMA

        def body(*refs):
            kernel(nd, nt, cx, cy, *refs)

        result = pl.pallas_call(
            body,
            out_shape=jax.ShapeDtypeStruct((4, cy, width), jnp.float32),
            in_specs=[
                pl.BlockSpec(memory_space=pl.ANY),
                pl.BlockSpec(memory_space=pltpu.SMEM),
                pl.BlockSpec(memory_space=pltpu.VMEM),
            ],
            out_specs=pl.BlockSpec(memory_space=pltpu.VMEM),
            scratch_shapes=[
                pltpu.VMEM((3, cx + 4, cy + 4, CHUNKS, LANES), jnp.float32),
                pltpu.VMEM((3, cx, cy, CHUNKS, LANES), jnp.float32),
                pltpu.VMEM((cx, cy, CHUNKS, LANES), jnp.float32),
                pltpu.VMEM((cx, cy, CHUNKS, LANES), jnp.float32),
                pltpu.VMEM((cx, cy - 4, CHUNKS, LANES), jnp.float32),
                pltpu.VMEM((2, cy - 12, CHUNKS, LANES), jnp.float32),
                pltpu.VMEM((2, 8, CHUNKS, LANES), jnp.float32),
                pltpu.VMEM((cx + 2, 3, CHUNKS, LANES), jnp.float32),
                pltpu.VMEM((cx + 2, 3, CHUNKS, LANES), jnp.float32),
                pltpu.VMEM((6 * LANES, 2 * LANES), jnp.bfloat16),
                pltpu.VMEM((6 * LANES, 2 * LANES), jnp.bfloat16),
                pltpu.VMEM((cx // 8, cy // 4, CHUNKS, LANES), jnp.float32),
                pltpu.VMEM((4, cy, CHUNKS, LANES), jnp.float32),
                pltpu.VMEM((2, nd // 2, 4, 2, cy, LANES), jnp.float32),
                pltpu.VMEM((nd // 2, 4, 2, cy, LANES), jnp.float32),
                pltpu.VMEM((nd // 2, 4, 2, cy, LANES), jnp.float32),
                dma((5,)),
                dma((2, 5)), dma((2, 5)), dma((2, 2)), dma((2, 2)),
                dma((18,)), dma((18,)), dma((cy // 8, nd)), dma((cy // 8, nd)), dma((cy // 8, nd)),
                dma((cy // 8, nd // 2)), dma((cy // 8, nd // 2)),
            ],
            compiler_params=pltpu.CompilerParams(
                collective_id=0, has_side_effects=True, vmem_limit_bytes=56 << 20
            ),
        )(velocity, view_sign, brick_flags)

        def hand_over(result_ref, color_ref, alpha_ref):
            color_ref[...] = result_ref[1:4]
            alpha_ref[...] = result_ref[0]

        return pl.pallas_call(
            hand_over,
            out_shape=(
                jax.ShapeDtypeStruct((3, cy, width), jnp.float32),
                jax.ShapeDtypeStruct((cy, width), jnp.float32),
            ),
        )(result)

    placed = (P(None, "depth", "tile", None), P("tile"), P("depth", "tile", None))
    return jax.shard_map(
        per_device,
        mesh=mesh,
        in_specs=placed,
        out_specs=(P(None, "tile", "depth"), P("tile", "depth")),
        check_vma=False,
    )
```

```python
import jax
import jax.numpy as jnp
from jax import lax
from jax.experimental import pallas as pl
from jax.experimental.pallas import tpu as pltpu
from jax.sharding import PartitionSpec as P

ALPHA_PEAK = 0.04
MESH = pl.DeviceIdType.MESH
LANES = 128
HALF = 8
CHUNKS = 2 * HALF


def split(value):
    high = value.astype(jnp.bfloat16)
    return high, (value - high.astype(jnp.float32)).astype(jnp.bfloat16)


def band_matrix(taps):
    shape = (6 * LANES, 2 * LANES)
    row = lax.broadcasted_iota(jnp.int32, shape, 0)
    lane = lax.rem(row, LANES)
    apart = jnp.where(lane < LANES // 2, lane + 2 * LANES, lane - LANES)
    cell = jnp.where(row < 4 * LANES, lax.rem(row, 2 * LANES), apart)
    offset = cell - lax.broadcasted_iota(jnp.int32, shape, 1)
    band = jnp.zeros(shape, jnp.float32)
    for at, weight in taps:
        band = jnp.where(offset == at, weight, band)
    return band.astype(jnp.bfloat16)


def along_z(value, band):
    lead = value.shape[:-2]
    flat = value.reshape((-1, CHUNKS, LANES))
    even, odd = flat[:, :HALF], flat[:, HALF:]
    lane = lax.broadcasted_iota(jnp.int32, even.shape, 2)
    sub = lax.broadcasted_iota(jnp.int32, even.shape, 1)
    beside = jnp.where(lane < 2, pltpu.roll(even, HALF - 1, 1), pltpu.roll(odd, 1, 1))
    outside = ((lane < 2) & (sub == HALF - 1)) | ((lane >= 2) & (sub == 0))
    beside = jnp.where(outside, 0.0, beside)
    parts = [split(v.reshape((-1, LANES))) for v in (even, odd, beside)]
    (e_hi, e_lo), (o_hi, o_lo), (b_hi, b_lo) = parts
    operand = jnp.concatenate([e_hi, o_hi, e_lo, o_lo, b_hi, b_lo], axis=1)
    out = jnp.dot(operand, band[...], preferred_element_type=jnp.float32)
    halves = [out[:, h * LANES : (h + 1) * LANES].reshape((-1, HALF, LANES)) for h in range(2)]
    return jnp.concatenate(halves, axis=1).reshape(lead + (CHUNKS, LANES))


def q_rows(u, gz, q, x, y, rows):
    def parts(comp):
        span = u[comp, x + 2, pl.ds(y, rows + 4)]
        near_x = u[comp, x + 3, pl.ds(y + 2, rows)] - u[comp, x + 1, pl.ds(y + 2, rows)]
        far_x = u[comp, x + 4, pl.ds(y + 2, rows)] - u[comp, x, pl.ds(y + 2, rows)]
        near_y = span[3 : rows + 3] - span[1 : rows + 1]
        far_y = span[4:] - span[:rows]
        return (
            8.0 * near_x - far_x,
            8.0 * near_y - far_y,
            gz[comp, x, pl.ds(y, rows)],
        )

    g00, g01, g02 = parts(0)
    total = g00 * g00
    g10, g11, g12 = parts(1)
    total = total + g11 * g11
    cross = g01 * g10
    g20, g21, g22 = parts(2)
    total = total + g22 * g22
    cross = cross + g02 * g20 + g12 * g21
    q[x, pl.ds(y, rows)] = total + (cross + cross)


def kernel(
    nd, nt, cx, cy, vel, sign, bricks, result,
    u, gz, glow, raw, q, face_a, face_b, q_low, q_high, slope, smoother, flags, image, near, merged, far, load_sem,
    xs_sem, xr_sem, ys_sem, yr_sem, qs_sem, qr_sem, is_sem, ir_sem, own_sem, fs_sem, fr_sem,
):
    depth, tile = lax.axis_index("depth"), lax.axis_index("tile")
    d_next, d_prev = lax.rem(depth + 1, nd), lax.rem(depth + nd - 1, nd)
    t_next, t_prev = lax.rem(tile + 1, nt), lax.rem(tile + nt - 1, nt)
    inner = cx - 4
    mid = cy - 4

    def load(group, x0, nx, y0, ny):
        for comp in range(3):
            for chunk in range(CHUNKS):
                pltpu.make_async_copy(
                    vel.at[comp, pl.ds(x0, nx), pl.ds(y0, ny), pl.ds(chunk * LANES, LANES)],
                    u.at[comp, pl.ds(x0 + 2, nx), pl.ds(y0 + 2, ny),
                         HALF * (chunk % 2) + chunk // 2],
                    load_sem.at[group],
                ).start()

    def loaded(group, x0, nx, y0, ny):
        where = u.at[:, pl.ds(x0 + 2, nx), pl.ds(y0 + 2, ny)]
        pltpu.make_async_copy(where, where, load_sem.at[group]).wait()

    faces = ((0, cx - 2, 2, 0, cy), (1, 0, 2, 0, cy))
    edges = ((2, 2, inner, 0, 8), (3, 2, inner, cy - 8, 8))
    middle = (4, 2, inner, 8, cy - 16)
    around = [(d_next, tile), (d_prev, tile), (depth, t_next), (depth, t_prev),
              (d_next, t_next), (d_next, t_prev), (d_prev, t_next), (d_prev, t_prev)]
    around += [(lax.rem(depth + hop, nd), tile) for hop in range(2, nd, 2)]
    barrier = pltpu.get_barrier_semaphore()
    for device in around:
        pl.semaphore_signal(barrier, inc=1, device_id=device, device_id_type=MESH)
    for group in faces + edges + (middle,):
        load(*group)
    pl.semaphore_wait(barrier, len(around))

    def send(src, dst, s_sem, r_sem, device):
        copy = pltpu.make_async_remote_copy(
            src_ref=src, dst_ref=dst, send_sem=s_sem, recv_sem=r_sem,
            device_id=device, device_id_type=MESH,
        )
        copy.start()
        return copy

    bands = ((2, cy - 12), (0, 2), (cy - 2, 2), (cy - 10, 8))
    for group in faces:
        loaded(*group)
    x_sends, y_sends = {}, {}

    def issue_x(b):
        y0, ny = bands[b]
        rows = pl.ds(y0 + 2, ny)
        x_sends[b] = (
            send(u.at[:, pl.ds(cx, 2), rows], u.at[:, pl.ds(0, 2), rows],
                 xs_sem.at[0, b], xr_sem.at[0, b], (d_next, tile)),
            send(u.at[:, pl.ds(2, 2), rows], u.at[:, pl.ds(cx + 2, 2), rows],
                 xs_sem.at[1, b], xr_sem.at[1, b], (d_prev, tile)),
        )

    half = cx // 2

    def issue_y(h):
        part_x = pl.ds(2 + h * half, half)
        y_sends[h] = (
            send(u.at[:, part_x, pl.ds(cy, 2)], u.at[:, part_x, pl.ds(0, 2)],
                 ys_sem.at[0, h], yr_sem.at[0, h], (depth, t_next)),
            send(u.at[:, part_x, pl.ds(2, 2)], u.at[:, part_x, pl.ds(cy + 2, 2)],
                 ys_sem.at[1, h], yr_sem.at[1, h], (depth, t_prev)),
        )

    for b in (0, 1, 2):
        issue_x(b)
    for group in edges:
        loaded(*group)
    issue_y(0)
    loaded(*middle)

    position = lax.broadcasted_iota(jnp.int32, (CHUNKS, CHUNKS), 0)
    wanted = 2 * lax.rem(position, HALF) + position // HALF
    pick = lax.broadcasted_iota(jnp.int32, (CHUNKS, CHUNKS), 1) == wanted
    half_peak = 0.5 * ALPHA_PEAK
    for bx in range(cx // 8):
        rows_of = bricks[bx]
        for by in range(cy // 4):
            line = rows_of[by : by + 1].astype(jnp.float32) * half_peak
            column = jnp.sum(
                jnp.where(pick, jnp.broadcast_to(line, (CHUNKS, CHUNKS)), 0.0),
                axis=1, keepdims=True,
            )
            flags[bx, by] = jnp.broadcast_to(column, (CHUNKS, LANES))

    slope[...] = band_matrix(((-2, 1.0), (-1, -8.0), (1, 8.0), (2, -1.0)))
    smoother[...] = band_matrix(((-1, 1.0), (0, 2.0), (1, 1.0)))
    own_y = pl.ds(2, cy)

    def z_plane(x, carry):
        for comp in range(3):
            gz[comp, x] = along_z(u[comp, x + 2, own_y], slope)
        return carry

    lax.fori_loop(0, cx, z_plane, 0)
    issue_x(3)
    issue_y(1)

    def glow_plane(x, carry):
        def speed(k, carry):
            rows = pl.ds(4 * k, 4)
            squares = [u[comp, x + 2, pl.ds(4 * k + 2, 4)] for comp in range(3)]
            squares = [v * v for v in squares]
            glow[x, rows] = jnp.tanh(0.5 * (squares[0] + squares[1] + squares[2]) - 1.5)
            return carry

        return lax.fori_loop(0, cy // 4, speed, carry)

    lax.fori_loop(0, cx, glow_plane, 0)
    big = 4

    def inside(step, carry):
        x = step + 2

        def block(k, carry):
            q_rows(u, gz, raw, x, 2 + big * k, big)
            return carry

        lax.fori_loop(0, mid // big, block, 0)
        q[x] = along_z(raw[x, pl.ds(2, mid)], smoother)
        return carry

    def face_x(i):
        return i + jnp.where(i >= 2, cx - 4, 0)

    q_sends, rim_sends = [], []

    def send_q(src, dst, device, into):
        k = len(q_sends) + len(rim_sends)
        into.append(send(src, dst, qs_sem.at[k], qr_sem.at[k], device))

    def x_arrived(b):
        y0, ny = bands[b]
        for copy in x_sends[b]:
            copy.wait_recv()

        @pl.when(depth == 0)
        def _():
            u[:, 0:2, y0 + 2 : y0 + 2 + ny] = jnp.zeros((3, 2, ny, CHUNKS, LANES), jnp.float32)

        @pl.when(depth == nd - 1)
        def _():
            u[:, cx + 2 : cx + 4, y0 + 2 : y0 + 2 + ny] = jnp.zeros(
                (3, 2, ny, CHUNKS, LANES), jnp.float32)

    def outside(b):
        y0, ny = bands[b]

        def block(step, carry):
            q_rows(u, gz, raw, face_x(step // (ny // big)), y0 + big * lax.rem(step, ny // big), big)
            return carry

        lax.fori_loop(0, 4 * (ny // big), block, 0)
        rows = pl.ds(y0 - 2, ny)
        for x0 in (0, cx - 2):
            q[pl.ds(x0, 2), rows] = along_z(raw[pl.ds(x0, 2), pl.ds(y0, ny)], smoother)
        face = face_a if b == 0 else face_b
        send_q(q.at[cx - 1, rows], face.at[0], (d_next, tile), q_sends)
        send_q(q.at[0, rows], face.at[1], (d_prev, tile), q_sends)

    def rim(h):
        for copy in y_sends[h]:
            copy.wait_recv()

        @pl.when(tile == 0)
        def _():
            u[:, 2 + h * half : 2 + h * half + half, 0:2] = jnp.zeros(
                (3, half, 2, CHUNKS, LANES), jnp.float32)

        @pl.when(tile == nt - 1)
        def _():
            u[:, 2 + h * half : 2 + h * half + half, cy + 2 : cy + 4] = jnp.zeros(
                (3, half, 2, CHUNKS, LANES), jnp.float32)

        def both(x, carry):
            q_rows(u, gz, raw, x, 0, 2)
            q_rows(u, gz, raw, x, cy - 2, 2)
            return carry

        lax.fori_loop(h * half, h * half + half, both, 0)
        own_q, own_raw = pl.ds(1 + h * half, half), pl.ds(h * half, half)
        q_low[own_q, 1:3] = along_z(raw[own_raw, 0:2], smoother)
        q_high[own_q, 0:2] = along_z(raw[own_raw, cy - 2 : cy], smoother)
        send_q(q_high.at[own_q, 1], q_low.at[own_q, 0], (depth, t_next), rim_sends)
        send_q(q_low.at[own_q, 1], q_high.at[own_q, 2], (depth, t_prev), rim_sends)
        at, to, device = (1, cx + 1, d_prev) if h == 0 else (cx, 0, d_next)
        send_q(q_low.at[at, pl.ds(1, 2)], q_low.at[to, pl.ds(1, 2)], (device, tile), rim_sends)
        send_q(q_high.at[at, pl.ds(0, 2)], q_high.at[to, pl.ds(0, 2)], (device, tile), rim_sends)
        send_q(q_high.at[at, 1], q_low.at[to, 0], (device, t_next), rim_sends)
        send_q(q_low.at[at, 1], q_high.at[to, 2], (device, t_prev), rim_sends)

    flip = sign[0]
    scale = -1.0 / (288.0 * 64.0)

    def along(view):
        return view + flip * (cx - 1 - 2 * view)

    def image_row(y):
        if isinstance(y, int):
            return y - 4 if 4 <= y < cy - 4 else (y + cy - 8 if y < 4 else y)
        return y - 4

    def composite(y, rows, span_of, unroll):
        def y_blurred(x, face=False):
            span = span_of(x, face)
            return (span[0:rows] + span[2 : rows + 2]) + 2.0 * span[1 : rows + 1]

        def shade_layer(x, after, state):
            before, here, trans, sum_a, sum_b, sum_c = state
            smooth = (before + after) + 2.0 * here
            peak = flags[x // 8, y // 4][None]
            tanh_q = jnp.tanh(scale * smooth)
            tanh_half = jnp.tanh((0.5 * scale) * smooth)
            tanh_speed = glow[x, pl.ds(y, rows)]
            weight = trans * (peak + peak * tanh_q)
            return (here, after, trans - weight, sum_a + weight * tanh_half,
                    sum_b + weight * tanh_speed, sum_c + weight * tanh_q)

        def layer(view, state):
            return shade_layer(along(view), y_blurred(along(view + 1)), state)

        one = jnp.ones((rows, CHUNKS, LANES), jnp.float32)
        zero = jnp.zeros((rows, CHUNKS, LANES), jnp.float32)
        state = (y_blurred(flip, True), y_blurred(along(0)), one, zero, zero, zero)
        state = lax.fori_loop(0, cx - 1, layer, state, unroll=unroll)
        state = shade_layer(along(cx - 1), y_blurred(1 - flip, True), state)
        _, _, trans, sum_a, sum_b, sum_c = state
        covered = 1.0 - trans
        where = pl.ds(image_row(y), rows)
        image[0, where] = trans
        image[1, where] = 0.5 * (covered + sum_a)
        image[2, where] = 0.5 * (covered + sum_b)
        image[3, where] = 0.5 * (covered - sum_c)

    def span_a(y):
        return lambda x, face: (face_a if face else q)[x, pl.ds(y - 3, 4)]

    def span_b(y):
        return lambda x, face: face_b[x, pl.ds(y - cy + 9, 4)] if face else q[x, pl.ds(y - 3, 4)]

    def span_ab(y):
        cut = cy - 10 - (y - 1)

        def span(x, face):
            if not face:
                return q[x, y - 3 : y + 1]
            return jnp.concatenate([face_a[x, y - 3 : y - 3 + cut], face_b[x, 0 : 4 - cut]], axis=0)

        return span

    def span_low(x, face):
        if face:
            return jnp.concatenate([q_low[x * (cx + 1)], face_a[x, 0:3]], axis=0)
        return jnp.concatenate([q_low[x + 1], q[x, 0:3]], axis=0)

    def span_high(x, face):
        if face:
            return jnp.concatenate([face_b[x, 5:8], q_high[x * (cx + 1)]], axis=0)
        return jnp.concatenate([q[x, mid - 3 : mid], q_high[x + 1]], axis=0)

    def row_pairs(y0, count, span):
        def pair(k, carry):
            y = y0 + 2 * k
            composite(y, 2, span(y), 5)
            return carry

        lax.fori_loop(0, count // 2, pair, 0)

    chip, core = depth // 2, lax.rem(depth, 2)
    chips = nd // 2
    hops = sorted(range(1, chips), key=lambda hop: abs(2 * hop - chips))

    def near_copies(group, core_at):
        rows = pl.ds(8 * group, 8)
        give, keep = [], []
        for to in range(chips):
            for par in range(2):
                k = 2 * to + par
                dst = near.at[core_at, to, :, par, rows]
                src = image.at[:, rows, HALF * par + 2 * to + (1 - core_at)]
                give.append(pltpu.make_async_remote_copy(
                    src_ref=src, dst_ref=dst, send_sem=is_sem.at[group, k],
                    recv_sem=ir_sem.at[group, k], device_id=(2 * chip + (1 - core_at), tile),
                    device_id_type=MESH))
                src = image.at[:, rows, HALF * par + 2 * to + core_at]
                keep.append(pltpu.make_async_copy(src, dst, own_sem.at[group, k]))
        return give, keep

    def send_near(group):
        for core_at in range(2):
            @pl.when(core == core_at)
            def _(core_at=core_at):
                for copies in near_copies(group, core_at):
                    for copy in copies:
                        copy.start()

    def far_copy(group, to, source):
        rows = pl.ds(8 * group, 8)
        return pltpu.make_async_remote_copy(
            src_ref=merged.at[to, :, :, rows], dst_ref=far.at[source, :, :, rows],
            send_sem=fs_sem.at[group, to], recv_sem=fr_sem.at[group, source],
            device_id=(2 * to + core, tile), device_id_type=MESH)

    def merge_near(group):
        for core_at in range(2):
            @pl.when(core == core_at)
            def _(core_at=core_at):
                for copies in near_copies(group, core_at):
                    for copy in copies:
                        copy.wait()
        rows = pl.ds(8 * group, 8)
        straight = flip == 0
        for to in range(chips):
            one, two = near[0, to, :, :, rows], near[1, to, :, :, rows]
            front, back = jnp.where(straight, one, two), jnp.where(straight, two, one)
            trans = front[0] * back[0]
            shade = front[1:] + front[0][None] * back[1:]
            merged[to, 0, :, rows] = trans
            merged[to, 1:4, :, rows] = shade

            @pl.when(chip == to)
            def _(to=to, trans=trans, shade=shade):
                far[to, 0, :, rows] = trans
                far[to, 1:4, :, rows] = shade
        for hop in hops:
            far_copy(group, lax.rem(chip + hop, chips), chip).start()

    def faces_arrived(copies, face):
        for copy in copies:
            copy.wait_recv()

        @pl.when(depth == 0)
        def _():
            face[0] = jnp.zeros(face.shape[1:], jnp.float32)

        @pl.when(depth == nd - 1)
        def _():
            face[1] = jnp.zeros(face.shape[1:], jnp.float32)

    lax.fori_loop(0, inner // 2, inside, 0)
    x_arrived(0)
    outside(0)
    x_arrived(1)
    x_arrived(2)
    rim(0)
    lax.fori_loop(inner // 2, inner, inside, 0)
    rim(1)
    x_arrived(3)
    outside(3)
    faces_arrived(q_sends[:2], face_a)
    row_pairs(4, 8, span_a)
    send_near(0)
    row_pairs(12, 8, span_a)
    send_near(1)
    merge_near(0)
    faces_arrived(q_sends[2:], face_b)
    composite(cy - 12, 2, span_ab(cy - 12), 5)
    composite(cy - 10, 2, span_ab(cy - 10), 5)
    row_pairs(cy - 8, 4, span_b)
    send_near(2)
    merge_near(1)

    for copy in rim_sends:
        copy.wait_recv()

    @pl.when(depth == 0)
    def _():
        q_low[0] = jnp.zeros((3, CHUNKS, LANES), jnp.float32)
        q_high[0] = jnp.zeros((3, CHUNKS, LANES), jnp.float32)

    @pl.when(depth == nd - 1)
    def _():
        q_low[cx + 1] = jnp.zeros((3, CHUNKS, LANES), jnp.float32)
        q_high[cx + 1] = jnp.zeros((3, CHUNKS, LANES), jnp.float32)

    @pl.when(tile == 0)
    def _():
        q_low[:, 0] = jnp.zeros((cx + 2, CHUNKS, LANES), jnp.float32)

    @pl.when(tile == nt - 1)
    def _():
        q_high[:, 2] = jnp.zeros((cx + 2, CHUNKS, LANES), jnp.float32)

    composite(0, 4, span_low, 3)
    composite(cy - 4, 4, span_high, 3)
    send_near(3)
    merge_near(2)
    merge_near(3)

    for group in range(4):
        for hop in hops:
            to = lax.rem(chip + hop, chips)
            far_copy(group, to, to).wait()

    trans = shade = None
    for view in range(chips):
        part = far[view + flip * (chips - 1 - 2 * view)]
        if trans is None:
            trans, shade = part[0], part[1:]
        else:
            shade = shade + trans[None] * part[1:]
            trans = trans * part[0]
    for par in range(2):
        lanes = slice(par * LANES, (par + 1) * LANES)
        for y0, at, ny in ((4, 0, cy - 8), (0, cy - 8, 4), (cy - 4, cy - 4, 4)):
            result[1:4, y0 : y0 + ny, lanes] = shade[:, par, at : at + ny]
            result[0, y0 : y0 + ny, lanes] = 1.0 - trans[par, at : at + ny]

    for pair in list(x_sends.values()) + list(y_sends.values()):
        for copy in pair:
            copy.wait_send()
    for copy in q_sends + rim_sends:
        copy.wait_send()


def solution(mesh):
    nd, nt = mesh.shape["depth"], mesh.shape["tile"]

    def per_device(velocity, view_sign, brick_flags):
        _, cx, cy, cz = velocity.shape
        width = cz // nd
        dma = pltpu.SemaphoreType.DMA

        def body(*refs):
            kernel(nd, nt, cx, cy, *refs)

        result = pl.pallas_call(
            body,
            out_shape=jax.ShapeDtypeStruct((4, cy, width), jnp.float32),
            in_specs=[
                pl.BlockSpec(memory_space=pl.ANY),
                pl.BlockSpec(memory_space=pltpu.SMEM),
                pl.BlockSpec(memory_space=pltpu.VMEM),
            ],
            out_specs=pl.BlockSpec(memory_space=pltpu.VMEM),
            scratch_shapes=[
                pltpu.VMEM((3, cx + 4, cy + 4, CHUNKS, LANES), jnp.float32),
                pltpu.VMEM((3, cx, cy, CHUNKS, LANES), jnp.float32),
                pltpu.VMEM((cx, cy, CHUNKS, LANES), jnp.float32),
                pltpu.VMEM((cx, cy, CHUNKS, LANES), jnp.float32),
                pltpu.VMEM((cx, cy - 4, CHUNKS, LANES), jnp.float32),
                pltpu.VMEM((2, cy - 12, CHUNKS, LANES), jnp.float32),
                pltpu.VMEM((2, 8, CHUNKS, LANES), jnp.float32),
                pltpu.VMEM((cx + 2, 3, CHUNKS, LANES), jnp.float32),
                pltpu.VMEM((cx + 2, 3, CHUNKS, LANES), jnp.float32),
                pltpu.VMEM((6 * LANES, 2 * LANES), jnp.bfloat16),
                pltpu.VMEM((6 * LANES, 2 * LANES), jnp.bfloat16),
                pltpu.VMEM((cx // 8, cy // 4, CHUNKS, LANES), jnp.float32),
                pltpu.VMEM((4, cy, CHUNKS, LANES), jnp.float32),
                pltpu.VMEM((2, nd // 2, 4, 2, cy, LANES), jnp.float32),
                pltpu.VMEM((nd // 2, 4, 2, cy, LANES), jnp.float32),
                pltpu.VMEM((nd // 2, 4, 2, cy, LANES), jnp.float32),
                dma((5,)),
                dma((2, 5)), dma((2, 5)), dma((2, 2)), dma((2, 2)),
                dma((18,)), dma((18,)), dma((cy // 8, nd)), dma((cy // 8, nd)), dma((cy // 8, nd)),
                dma((cy // 8, nd // 2)), dma((cy // 8, nd // 2)),
            ],
            compiler_params=pltpu.CompilerParams(
                collective_id=0, has_side_effects=True, vmem_limit_bytes=56 << 20
            ),
        )(velocity, view_sign, brick_flags)

        def hand_over(result_ref, color_ref, alpha_ref):
            color_ref[...] = result_ref[1:4]
            alpha_ref[...] = result_ref[0]

        return pl.pallas_call(
            hand_over,
            out_shape=(
                jax.ShapeDtypeStruct((3, cy, width), jnp.float32),
                jax.ShapeDtypeStruct((cy, width), jnp.float32),
            ),
        )(result)

    placed = (P(None, "depth", "tile", None), P("tile"), P("depth", "tile", None))
    return jax.shard_map(
        per_device,
        mesh=mesh,
        in_specs=placed,
        out_specs=(P(None, "tile", "depth"), P("tile", "depth")),
        check_vma=False,
    )
```
